256 devices in a mesh: az: 128 (over z, y, x_hi, core), rd: 2 (over x_lo).
Axes of the slice: x: 4 (x_hi: 2, x_lo: 2; x = x_hi * 2 + x_lo), y: 4, z: 8, core: 2. Of those that a mesh axis runs over, the one named last changes fastest.
Arguments:
- echoes: bfloat16 [2, 2048, 32, 2048], P(None, 'az', None, 'rd'), may hold values from -6 to 6
- pulse_taper: float32 [32], replicated, may hold values from 0.1 to 1.9
- beam_weights: float32 [5], replicated, may hold values from 0.3 to 1
- blanking: int32 [2048, 16], P('az'), may hold values 0 or 1
- cfar_sizes: int32 [6], replicated, may hold values from 1 to 23, as said below
Outputs:
- detection: bfloat16 [2048, 32, 2048], P('az', 'rd')
The draws below stay inside these ranges and needn't reach their ends.
Inputs may be any that keep to these rules, and one draw needn't show every extreme that they name: `cfar_sizes`: the range guard (entry 0) is 1; the Doppler and azimuth guards (entries 2, 4) are 1 or 2; guard plus window is exactly 24 for range (entries 0, 1), 4 for Doppler (2, 3) and 12 for azimuth (4, 5).
All inputs are finite; a program needn't handle non-finite values. No bound on the sum of `blanking` on one device may be relied on, other than what follows from the above.
Results may differ from the reference program's by a relative error of at most 0.012.
Values may be sent and summed in bfloat16 or wider, within the bound.
A program may use at most 64 MiB of HBM per device.

```python
import math
import jax
import jax.numpy as jnp
from jax import lax

PULSES = 32
AZ_DEV = 16
REACH_R = 24
REACH_D = 4
REACH_A = 12
BLANK_CELLS = 128
AZ = 2048
RANGE = 2048
RBLK = 16


def draw_cfar_sizes(key, part):
    others = jax.random.randint(jax.random.fold_in(key, 11), (2,), 1, 3).astype(jnp.int32)
    guards = jnp.concatenate([jnp.ones((1,), dtype=jnp.int32), others]).astype(jnp.int32)
    reaches = jnp.array([REACH_R, REACH_D, REACH_A], dtype=jnp.int32)
    windows = reaches - guards
    return jnp.stack([guards, windows], axis=1).reshape(6).astype(jnp.int32)


def plant(values, key, smallest, largest):
    longest = values.shape.index(max(values.shape))
    spots = []
    for shift in (0, 1):
        where = [jax.random.randint(jax.random.fold_in(key, axis), (), 0, length) for axis, length in enumerate(values.shape)]
        where[longest] = (where[longest] + shift) % values.shape[longest]
        spots.append(tuple(where))
    return values.at[spots[0]].set(smallest).at[spots[1]].set(largest)


def level_of(stream_key, dims, cuts, low, high):
    loudness, own = 1.0, jax.random.fold_in(stream_key, 6)
    for axis_at, parts in cuts:
        steps = jnp.exp(jax.random.uniform(jax.random.fold_in(own, axis_at), (parts,), jnp.float32, low / len(cuts), high / len(cuts)))
        loudness = loudness * jnp.repeat(steps, dims[axis_at] // parts).reshape([-1 if axis == axis_at else 1 for axis in range(len(dims))])
    return loudness


def noise(own_key, dims, spread, most, split=(), held_as=jnp.bfloat16):
    level = level_of(own_key, dims, split, -0.22, 0.18) if split else 1.0
    drawn = jax.random.normal(own_key, dims, jnp.float32) * spread * level
    return jnp.minimum(jnp.maximum(drawn, -most), most).astype(held_as)


def setup_inputs(seed: int = 0) -> dict:
    key_of = jax.random.split(jax.random.key(seed), 6)
    return {
        "echoes": noise(key_of[0], (2, AZ, PULSES, RANGE), 1.0, 6.0, ((1, 128), (3, 2))),
        "pulse_taper": jnp.clip(1.0 + 0.18 * jax.random.normal(key_of[1], (PULSES,), jnp.float32), 0.1, 1.9),
        "beam_weights": jnp.clip(jax.random.uniform(key_of[2], (5,), jnp.float32, 0.3, 1.0), 0.3, 1.0),
        "blanking": plant((jax.random.randint(key_of[3], (AZ, RBLK), 0, 4) < 3).astype(jnp.int32), jax.random.fold_in(key_of[3], 1), 0, 1),
        "cfar_sizes": draw_cfar_sizes(jax.random.fold_in(key_of[5], 71), 0),
    }


def bank_matrix(pulse_taper):
    pulses = pulse_taper.shape[0]
    indices = jnp.arange(pulses, dtype=jnp.int32)
    phases = (indices[:, None] * indices[None, :]) % pulses
    angles = phases.astype(jnp.float32) * (2.0 * math.pi / pulses)
    cosines = jnp.cos(angles) * pulse_taper[None, :]
    sine_terms = jnp.sin(angles) * pulse_taper[None, :]
    real_row = jnp.stack([cosines, sine_terms], axis=1)
    imag_row = jnp.stack([-sine_terms, cosines], axis=1)
    return jnp.stack([real_row, imag_row], axis=0).astype(jnp.bfloat16)


def dwell_block(block_index, echoes, bank, beam_weights, blanking, cfar_sizes):
    first = (block_index * AZ_DEV).astype(jnp.int32)
    dwell_ids = (first - REACH_A - 2 + jnp.arange(AZ_DEV + 2 * REACH_A + 4, dtype=jnp.int32)) % AZ
    selected = jnp.take(echoes, dwell_ids, axis=1).astype(jnp.float32)
    spectrum = jnp.einsum("ckdp,dapr->cakr", bank.astype(jnp.float32), selected, precision=lax.Precision.HIGHEST)
    powers = (spectrum[0] * spectrum[0] + spectrum[1] * spectrum[1]) / PULSES
    span = AZ_DEV + 2 * REACH_A
    integrated = beam_weights[0] * powers[0:span]
    for offset in range(1, 5):
        integrated = integrated + beam_weights[offset] * powers[offset:offset + span]
    log_power = jnp.log(integrated + 0.05).astype(jnp.bfloat16).astype(jnp.float32)
    center = log_power[REACH_A:REACH_A + AZ_DEV]
    guard_range = cfar_sizes[0]
    window_doppler = cfar_sizes[3].astype(jnp.float32)
    guard_doppler = cfar_sizes[2]
    guard_azimuth = cfar_sizes[4]
    window_azimuth = cfar_sizes[5].astype(jnp.float32)

    azimuth_lead = jnp.zeros_like(center)
    azimuth_lag = jnp.zeros_like(center)
    for offset in range(1, REACH_A + 1):
        chosen = (offset > guard_azimuth).astype(jnp.float32)
        azimuth_lead = azimuth_lead + chosen * log_power[REACH_A - offset:REACH_A - offset + AZ_DEV]
        azimuth_lag = azimuth_lag + chosen * log_power[REACH_A + offset:REACH_A + offset + AZ_DEV]
    azimuth_lead = azimuth_lead / window_azimuth
    azimuth_lag = azimuth_lag / window_azimuth

    rows_kept = lax.dynamic_slice_in_dim(blanking, first, AZ_DEV, 0).astype(jnp.float32)
    weight = jnp.repeat(rows_kept, BLANK_CELLS, axis=1)
    weighted = center * weight[:, None, :]
    padded_values = jnp.pad(weighted, ((0, 0), (0, 0), (REACH_R, REACH_R)))
    padded_weight = jnp.pad(weight, ((0, 0), (REACH_R, REACH_R)))
    lead_sum = jnp.zeros_like(center)
    lag_sum = jnp.zeros_like(center)
    lead_count = jnp.zeros_like(weight)
    lag_count = jnp.zeros_like(weight)
    for offset in range(1, REACH_R + 1):
        chosen = (offset > guard_range).astype(jnp.float32)
        lead_sum = lead_sum + chosen * padded_values[:, :, REACH_R - offset:REACH_R - offset + RANGE]
        lag_sum = lag_sum + chosen * padded_values[:, :, REACH_R + offset:REACH_R + offset + RANGE]
        lead_count = lead_count + chosen * padded_weight[:, REACH_R - offset:REACH_R - offset + RANGE]
        lag_count = lag_count + chosen * padded_weight[:, REACH_R + offset:REACH_R + offset + RANGE]
    range_lead = lead_sum / jnp.maximum(lead_count, 1.0)[:, None, :]
    range_lag = lag_sum / jnp.maximum(lag_count, 1.0)[:, None, :]

    doppler_lead = jnp.zeros_like(center)
    doppler_lag = jnp.zeros_like(center)
    for offset in range(1, REACH_D + 1):
        chosen = (offset > guard_doppler).astype(jnp.float32)
        doppler_lead = doppler_lead + chosen * jnp.roll(center, offset, axis=1)
        doppler_lag = doppler_lag + chosen * jnp.roll(center, -offset, axis=1)
    doppler_lead = doppler_lead / window_doppler
    doppler_lag = doppler_lag / window_doppler

    noise_level = jnp.maximum(jnp.maximum(range_lead, range_lag), jnp.maximum(doppler_lead, doppler_lag))
    noise_level = jnp.maximum(noise_level, jnp.maximum(azimuth_lead, azimuth_lag))
    return (weight[:, None, :] * (center - noise_level)).astype(jnp.bfloat16)


def reference(echoes, pulse_taper, beam_weights, blanking, cfar_sizes):
    bank = bank_matrix(pulse_taper)
    blocks = jnp.arange(AZ // AZ_DEV, dtype=jnp.int32)
    result = lax.map(lambda number: dwell_block(number, echoes, bank, beam_weights, blanking, cfar_sizes), blocks)
    return result.reshape(AZ, PULSES, RANGE)
```

```python
import math

import jax
import jax.numpy as jnp
import numpy as np
from jax import lax
from jax.experimental import pallas as pl
from jax.experimental.pallas import tpu as pltpu
from jax.sharding import PartitionSpec as P

F32 = jnp.float32
BF16 = jnp.bfloat16
PULSES = 32
ROWS = 16
BINS = 16
LANES = 128
BLOCKS = 16
OWN = 8
CHUNKS = 4
PER = OWN // CHUNKS
WIDE = PER * LANES
REACH_R = 24
REACH_D = 4
REACH_A = 12
HALO = REACH_A + 2
SPAN = ROWS + 2 * REACH_A
ORDER = (0, 1, 2, 3, 12, 13, 14, 15, 4, 5, 6, 7, 8, 9, 10, 11)
EDGE = 8
KINDS = 10


def trig_table():
    bins = np.array([half * BINS + place for half in range(2) for place in ORDER])
    theta = 2.0 * np.pi * (np.outer(bins, np.arange(PULSES)) % PULSES) / PULSES
    cosines, sines = np.cos(theta), np.sin(theta)
    real = np.concatenate([cosines, sines], axis=1)
    imag = np.concatenate([-sines, cosines], axis=1)
    return np.concatenate([real, imag], axis=0).astype(np.float32)


def range_band():
    source = np.arange(3 * LANES)[:, None] - LANES
    lane = np.arange(LANES)[None, :]
    lead, lag = lane - source, source - lane
    bands = [((d > 1) & (d <= REACH_R)) for d in (lead, lag)]
    return np.concatenate(bands, axis=1).astype(np.float32)


def doppler_bands(group):
    tables = []
    for offsets in ((3, 4), (2,)):
        table = np.zeros((2, group, BINS, group * (BINS + EDGE)), np.float32)
        for side, sign in enumerate((-1, 1)):
            for row in range(group):
                for slot, place in enumerate(ORDER):
                    for offset in offsets:
                        source = (place + sign * offset) % PULSES
                        spot = ORDER.index(source % BINS)
                        if source < BINS:
                            column = row * BINS + spot
                        else:
                            column = group * BINS + row * EDGE + spot
                        table[side, row, slot, column] += 1.0
        tables.append(table.reshape(2 * group * BINS, -1))
    return tables


GROUP = 8


def kernel(
    echoes,
    taper,
    trig,
    band,
    dop_far,
    dop_near,
    beam,
    blank,
    cfar,
    out,
    held,
    power,
    off,
    off_edge,
    on,
    on_edge,
    logs,
    logs_edge,
    center,
    weighted,
    level,
    inverse,
    load_sem,
    send_sem,
    recv_sem,
):
    az, rd = lax.axis_index("az"), lax.axis_index("rd")
    count = lax.axis_size("az")
    odd = lax.rem(az, 2)
    pair = (az, 1 - rd)
    outer = (lax.rem(az - 1 + 2 * odd + count, count), 1 - rd)
    inner = (az + 1 - 2 * odd, rd)

    def physical(row):
        return row + odd * (ROWS - 1 - 2 * row)

    loads = []
    for c in range(CHUNKS):
        load = pltpu.make_async_copy(
            echoes.at[:, :, :, pl.ds(c * WIDE, WIDE)], held.at[c], load_sem.at[c]
        )
        load.start()
        loads.append(load)

    barrier = pltpu.get_barrier_semaphore()
    for target in (pair, outer, inner):
        pl.semaphore_signal(
            barrier, inc=1, device_id=target, device_id_type=pl.DeviceIdType.MESH
        )

    def transfer(c, kind, half):
        blocks = pl.ds(half * OWN + c * PER, PER)
        what = kind if kind < 2 else (kind - 2) % 4 + 2
        if what == 0:
            src, dst, target = power.at[0, blocks], power.at[1, blocks], pair
        elif what == 1:
            src, dst, target = power.at[1, blocks], power.at[0, blocks], pair
        elif what == 2:
            src, dst, target = power.at[1, blocks, pl.ds(0, HALO)], off.at[blocks], outer
        elif what == 3:
            src = power.at[0, blocks, pl.ds(0, 2), pl.ds(0, EDGE)]
            dst, target = off_edge.at[blocks], outer
        elif what == 4:
            src = power.at[0, blocks, pl.ds(ROWS - HALO, HALO)]
            dst, target = on.at[blocks], inner
        else:
            src = power.at[1, blocks, pl.ds(ROWS - 2, 2), pl.ds(0, EDGE)]
            dst, target = on_edge.at[blocks], inner
        return pltpu.make_async_remote_copy(
            src_ref=src,
            dst_ref=dst,
            send_sem=send_sem.at[c, kind],
            recv_sem=recv_sem.at[c, kind],
            device_id=target,
            device_id_type=pl.DeviceIdType.MESH,
        )

    sent = []

    def send(c, kind):
        copy = transfer(c, kind, rd if kind < 6 else 1 - rd)
        copy.start()
        sent.append(copy)

    def receive(c, kind):
        half = 1 - rd if kind in (0, 1, 2, 3, 8, 9) else rd
        transfer(c, kind, half).wait_recv()

    lane_parity = lax.rem(lax.broadcasted_iota(jnp.int32, (1, PULSES), 1), 2)
    signs = 1.0 - (2 * rd * lane_parity).astype(F32)
    tapered = taper[...] * signs
    bank = (trig[...] * jnp.concatenate([tapered, tapered], axis=1)).astype(BF16)

    for c in range(CHUNKS):
        loads[c].wait()
        for row in range(ROWS):
            spot = physical(row)
            pulses = jnp.concatenate([held[c, 0, spot], held[c, 1, spot]], axis=0)
            spectrum = jnp.dot(bank, pulses, preferred_element_type=F32)
            real, imag = spectrum[:PULSES], spectrum[PULSES:]
            powers = (real * real + imag * imag).astype(BF16)
            for part in range(PER):
                for half in range(2):
                    power[half, rd * OWN + c * PER + part, row] = powers[
                        half * BINS : (half + 1) * BINS, part * LANES : (part + 1) * LANES
                    ]
        if c == 0:
            pl.semaphore_wait(barrier, 3)
        for kind in (0, 1, 2, 3, 4, 5):
            send(c, kind)

    beams = [
        (beam[j] + odd.astype(F32) * (beam[4 - j] - beam[j])) * (1.0 / PULSES)
        for j in range(5)
    ]
    near_d = (2 - cfar[2]).astype(F32)
    near_a = (2 - cfar[4]).astype(F32)
    ones = jnp.ones((8, LANES), F32)
    scale_d = 1.0 / (ones * cfar[3].astype(F32))
    scale_d = jnp.concatenate([scale_d, scale_d], axis=0)
    scale_a = 1.0 / (ones * cfar[5].astype(F32))
    scale_a = jnp.concatenate([scale_a, scale_a], axis=0)
    doppler = (dop_far[...].astype(F32) + near_d * dop_near[...].astype(F32)).astype(BF16)

    lanes = lax.broadcasted_iota(jnp.int32, (8, LANES), 1)
    window = REACH_R - 1
    lead_in = jnp.clip(lanes - 1, 0, window).astype(F32)
    lag_in = jnp.clip(LANES - 2 - lanes, 0, window).astype(F32)
    lead_out, lag_out = window - lead_in, window - lag_in

    def weight_of(row, b):
        return blank[physical(row), b].astype(F32)

    @pl.loop(0, ROWS)
    def _(row):
        weights = [weight_of(row, b) for b in range(BLOCKS)]
        for b in range(BLOCKS):
            lead, lag = weights[b] * lead_in, weights[b] * lag_in
            if b > 0:
                lead = lead + weights[b - 1] * lead_out
            if b < BLOCKS - 1:
                lag = lag + weights[b + 1] * lag_out
            inverse[0, b, row] = 1.0 / jnp.maximum(lead, 1.0)
            inverse[1, b, row] = 1.0 / jnp.maximum(lag, 1.0)

    for edge in (0, BLOCKS + 1):
        weighted[edge] = jnp.zeros((ROWS, BINS, LANES), BF16)

    def integrate(rows, put):
        held_rows = [rows(e) for e in range(4)]
        last = None
        for t in range(put.count):
            held_rows.append(rows(t + 4))
            total = beams[0] * held_rows[0]
            for j in range(1, 5):
                total = total + beams[j] * held_rows[j]
            put(t, jnp.log(total + 0.05))
            held_rows.pop(0)

    def level_block(b):
        def rows(e):
            if e < HALO:
                return off[b, HALO - 1 - e].astype(F32)
            if e < HALO + ROWS:
                return power[0, b, e - HALO].astype(F32)
            return on[b, 2 * HALO + ROWS - 1 - e].astype(F32)

        def put(t, value):
            logs[t] = value
            row = t - REACH_A
            if 0 <= row < ROWS:
                rounded = value.astype(BF16)
                center[b, row] = rounded
                weighted[b + 1, row] = (
                    rounded.astype(F32) * weight_of(row, b)
                ).astype(BF16)

        put.count = SPAN
        integrate(rows, put)

        def edge_rows(e):
            if e < 2:
                return off_edge[b, 1 - e].astype(F32)
            if e < 2 + ROWS:
                return power[1, b, e - 2, 0:EDGE].astype(F32)
            return on_edge[b, 1 - (e - 2 - ROWS)].astype(F32)

        waiting = []

        def put_edge(t, value):
            waiting.append(value)
            if t % 2 == 1:
                logs_edge[t // 2] = jnp.concatenate(waiting, axis=0).astype(BF16)
                waiting.clear()

        put_edge.count = ROWS
        integrate(edge_rows, put_edge)

        means = []
        for group in range(ROWS // GROUP):
            stacked = jnp.concatenate(
                [
                    center[b, group * GROUP : (group + 1) * GROUP].reshape(
                        GROUP * BINS, LANES
                    ),
                    logs_edge[group * GROUP // 2 : (group + 1) * GROUP // 2].reshape(
                        GROUP * EDGE, LANES
                    ),
                ],
                axis=0,
            )
            sums = jnp.dot(doppler, stacked, preferred_element_type=F32)
            size = GROUP * BINS
            means.append(jnp.maximum(sums[:size], sums[size:]))

        far = REACH_A - 2
        lead = logs[0]
        lag = logs[REACH_A + 3]
        for d in range(1, far):
            lead = lead + logs[d]
            lag = lag + logs[REACH_A + 3 + d]
        for row in range(ROWS):
            azimuth = jnp.maximum(
                lead + near_a * logs[row + far], lag + near_a * logs[row + REACH_A + 2]
            )
            local = row % GROUP
            mean = means[row // GROUP][local * BINS : (local + 1) * BINS]
            level[b, row] = jnp.maximum(azimuth * scale_a, mean * scale_d)
            if row < ROWS - 1:
                lead = lead + (logs[row + far] - logs[row])
                lag = lag + (logs[row + REACH_A + 3 + far] - logs[row + REACH_A + 3])

    low = lax.broadcasted_iota(jnp.int32, (8, LANES), 0) < 4

    def finish_block(b):
        stacked = jnp.concatenate(
            [weighted[b + i].reshape(ROWS * BINS, LANES) for i in range(3)], axis=1
        )
        sums = jnp.dot(stacked, band[...], preferred_element_type=F32)
        cells = pl.ds(pl.multiple_of(b * LANES, LANES), LANES)
        for row in range(ROWS):
            here = slice(row * BINS, (row + 1) * BINS)
            lead, lag = inverse[0, b, row], inverse[1, b, row]
            lead = sums[here, :LANES] * jnp.concatenate([lead, lead], axis=0)
            lag = sums[here, LANES:] * jnp.concatenate([lag, lag], axis=0)
            noise = jnp.maximum(jnp.maximum(lead, lag), level[b, row])
            excess = weight_of(row, b) * (center[b, row].astype(F32) - noise)
            first, second = excess[:8], pltpu.roll(excess[8:], 4, 0)
            ordered = jnp.concatenate(
                [jnp.where(low, first, second), jnp.where(low, second, first)], axis=0
            )
            out[physical(row), :, cells] = ordered.astype(BF16)

    def blocks_of(first, size, body):
        @pl.loop(0, 2 * size)
        def _(index):
            body(lax.div(index, size) * OWN + first + lax.rem(index, size))

    def process(c):
        for kind in (2, 3, 4, 5, 6, 7, 8, 9):
            receive(c, kind)
        blocks_of(c * PER, PER, level_block)
        if c == 0:
            finish_block(0)
        elif c < CHUNKS - 1:
            blocks_of(c * PER - 1, PER, finish_block)
        else:
            blocks_of(c * PER - 1, PER + 1, finish_block)
            finish_block(OWN)

    for c in range(CHUNKS):
        receive(c, 0)
        receive(c, 1)
        for kind in (6, 7, 8, 9):
            send(c, kind)
        if c > 0:
            process(c - 1)
    process(CHUNKS - 1)

    for copy in sent:
        copy.wait_send()


def local(echoes, pulse_taper, beam_weights, blanking, cfar_sizes):
    far, near = doppler_bands(GROUP)
    vmem = pl.BlockSpec(memory_space=pltpu.VMEM)
    smem = pl.BlockSpec(memory_space=pltpu.SMEM)
    return pl.pallas_call(
        kernel,
        out_shape=jax.ShapeDtypeStruct((ROWS, BINS, BLOCKS * LANES), BF16),
        in_specs=[pl.BlockSpec(memory_space=pl.ANY)] + [vmem] * 5 + [smem] * 3,
        out_specs=vmem,
        scratch_shapes=[
            pltpu.VMEM((CHUNKS, 2, ROWS, PULSES, WIDE), BF16),
            pltpu.VMEM((2, BLOCKS, ROWS, BINS, LANES), BF16),
            pltpu.VMEM((BLOCKS, HALO, BINS, LANES), BF16),
            pltpu.VMEM((BLOCKS, 2, EDGE, LANES), BF16),
            pltpu.VMEM((BLOCKS, HALO, BINS, LANES), BF16),
            pltpu.VMEM((BLOCKS, 2, EDGE, LANES), BF16),
            pltpu.VMEM((SPAN, BINS, LANES), F32),
            pltpu.VMEM((ROWS // 2, BINS, LANES), BF16),
            pltpu.VMEM((BLOCKS, ROWS, BINS, LANES), BF16),
            pltpu.VMEM((BLOCKS + 2, ROWS, BINS, LANES), BF16),
            pltpu.VMEM((BLOCKS, ROWS, BINS, LANES), F32),
            pltpu.VMEM((2, BLOCKS, ROWS, 8, LANES), F32),
            pltpu.SemaphoreType.DMA((CHUNKS,)),
            pltpu.SemaphoreType.DMA((CHUNKS, KINDS)),
            pltpu.SemaphoreType.DMA((CHUNKS, KINDS)),
        ],
        compiler_params=pltpu.CompilerParams(
            collective_id=0, has_side_effects=True, vmem_limit_bytes=48 << 20
        ),
    )(
        echoes,
        pulse_taper.reshape(1, PULSES),
        jnp.asarray(trig_table()),
        jnp.asarray(range_band(), BF16),
        jnp.asarray(far, BF16),
        jnp.asarray(near, BF16),
        beam_weights,
        blanking,
        cfar_sizes,
    )


def solution(mesh):
    in_specs = (P(None, "az", None, "rd"), P(), P(), P("az", None), P())
    out_specs = P("az", "rd", None)
    return jax.shard_map(local, mesh=mesh, in_specs=in_specs, out_specs=out_specs, check_vma=False)
```

```python
import math

import jax
import jax.numpy as jnp
import numpy as np
from jax import lax
from jax.experimental import pallas as pl
from jax.experimental.pallas import tpu as pltpu
from jax.sharding import PartitionSpec as P

F32 = jnp.float32
BF16 = jnp.bfloat16
PULSES = 32
ROWS = 16
BINS = 16
LANES = 128
BLOCKS = 16
OWN = 8
CHUNKS = 4
PER = OWN // CHUNKS
WIDE = PER * LANES
REACH_R = 24
REACH_D = 4
REACH_A = 12
HALO = REACH_A + 2
SPAN = ROWS + 2 * REACH_A
ORDER = (0, 1, 2, 3, 12, 13, 14, 15, 4, 5, 6, 7, 8, 9, 10, 11)
EDGE = 8
KINDS = 10


def trig_table():
    bins = np.array([half * BINS + place for half in range(2) for place in ORDER])
    theta = 2.0 * np.pi * (np.outer(bins, np.arange(PULSES)) % PULSES) / PULSES
    cosines, sines = np.cos(theta), np.sin(theta)
    real = np.concatenate([cosines, sines], axis=1)
    imag = np.concatenate([-sines, cosines], axis=1)
    return np.concatenate([real, imag], axis=0).astype(np.float32)


def range_band():
    source = np.arange(3 * LANES)[:, None] - LANES
    lane = np.arange(LANES)[None, :]
    lead, lag = lane - source, source - lane
    bands = [((d > 1) & (d <= REACH_R)) for d in (lead, lag)]
    return np.concatenate(bands, axis=1).astype(np.float32)


def doppler_bands(group):
    tables = []
    for offsets in ((3, 4), (2,)):
        table = np.zeros((2, group, BINS, group * (BINS + EDGE)), np.float32)
        for side, sign in enumerate((-1, 1)):
            for row in range(group):
                for slot, place in enumerate(ORDER):
                    for offset in offsets:
                        source = (place + sign * offset) % PULSES
                        spot = ORDER.index(source % BINS)
                        if source < BINS:
                            column = row * BINS + spot
                        else:
                            column = group * BINS + row * EDGE + spot
                        table[side, row, slot, column] += 1.0
        tables.append(table.reshape(2 * group * BINS, -1))
    return tables


GROUP = 8


def kernel(
    echoes,
    *refs,
):
    sources, (result, *scratch) = refs[:8], refs[8:]
    tables, (stage_sem, *scratch) = scratch[:8], scratch[8:]
    stages = []
    for index, (source, table) in enumerate(zip(sources, tables)):
        stage = pltpu.make_async_copy(source, table, stage_sem.at[index])
        stages.append(stage)
    body(echoes, result, stages, *tables, *scratch)


def body(
    echoes,
    result,
    stages,
    taper,
    trig,
    band,
    dop_far,
    dop_near,
    beam,
    blank,
    cfar,
    out,
    held,
    power,
    off,
    off_edge,
    on,
    on_edge,
    logs,
    logs_edge,
    center,
    weighted,
    level,
    inverse,
    load_sem,
    send_sem,
    recv_sem,
    out_sem,
):
    az, rd = lax.axis_index("az"), lax.axis_index("rd")
    count = lax.axis_size("az")
    odd = lax.rem(az, 2)
    pair = (az, 1 - rd)
    outer = (lax.rem(az - 1 + 2 * odd + count, count), 1 - rd)
    inner = (az + 1 - 2 * odd, rd)

    def physical(row):
        return row + odd * (ROWS - 1 - 2 * row)

    loads = []
    for c in range(CHUNKS):
        load = pltpu.make_async_copy(
            echoes.at[:, :, :, pl.ds(c * WIDE, WIDE)], held.at[c], load_sem.at[c]
        )
        loads.append(load)
    for stage in stages[:2]:
        stage.start()
    for load in loads:
        load.start()
    for stage in stages[2:]:
        stage.start()

    barrier = pltpu.get_barrier_semaphore()
    for target in (pair, outer, inner):
        pl.semaphore_signal(
            barrier, inc=1, device_id=target, device_id_type=pl.DeviceIdType.MESH
        )

    def transfer(c, kind, half):
        blocks = pl.ds(half * OWN + c * PER, PER)
        what = kind if kind < 2 else (kind - 2) % 4 + 2
        if what == 0:
            src, dst, target = power.at[0, blocks], power.at[1, blocks], pair
        elif what == 1:
            src, dst, target = power.at[1, blocks], power.at[0, blocks], pair
        elif what == 2:
            src, dst, target = power.at[1, blocks, pl.ds(0, HALO)], off.at[blocks], outer
        elif what == 3:
            src = power.at[0, blocks, pl.ds(0, 2), pl.ds(0, EDGE)]
            dst, target = off_edge.at[blocks], outer
        elif what == 4:
            src = power.at[0, blocks, pl.ds(ROWS - HALO, HALO)]
            dst, target = on.at[blocks], inner
        else:
            src = power.at[1, blocks, pl.ds(ROWS - 2, 2), pl.ds(0, EDGE)]
            dst, target = on_edge.at[blocks], inner
        return pltpu.make_async_remote_copy(
            src_ref=src,
            dst_ref=dst,
            send_sem=send_sem.at[c, kind],
            recv_sem=recv_sem.at[c, kind],
            device_id=target,
            device_id_type=pl.DeviceIdType.MESH,
        )

    sent = []

    def send(c, kind):
        copy = transfer(c, kind, rd if kind < 6 else 1 - rd)
        copy.start()
        sent.append(copy)

    def receive(c, kind):
        half = 1 - rd if kind in (0, 1, 2, 3, 8, 9) else rd
        transfer(c, kind, half).wait_recv()

    for stage in stages[:2]:
        stage.wait()
    lane_parity = lax.rem(lax.broadcasted_iota(jnp.int32, (1, PULSES), 1), 2)
    signs = 1.0 - (2 * rd * lane_parity).astype(F32)
    tapered = taper[...] * signs
    bank = (trig[...] * jnp.concatenate([tapered, tapered], axis=1)).astype(BF16)

    for c in range(CHUNKS):
        loads[c].wait()
        for row in range(ROWS):
            spot = physical(row)
            pulses = jnp.concatenate([held[c, 0, spot], held[c, 1, spot]], axis=0)
            spectrum = jnp.dot(bank, pulses, preferred_element_type=F32)
            real, imag = spectrum[:PULSES], spectrum[PULSES:]
            powers = (real * real + imag * imag).astype(BF16)
            for part in range(PER):
                for half in range(2):
                    power[half, rd * OWN + c * PER + part, row] = powers[
                        half * BINS : (half + 1) * BINS, part * LANES : (part + 1) * LANES
                    ]
        if c == 0:
            pl.semaphore_wait(barrier, 3)
        for kind in (0, 1, 2, 3, 4, 5):
            send(c, kind)

    for stage in stages[2:]:
        stage.wait()
    beams = [
        (beam[j] + odd.astype(F32) * (beam[4 - j] - beam[j])) * (1.0 / PULSES)
        for j in range(5)
    ]
    near_d = (2 - cfar[2]).astype(F32)
    near_a = (2 - cfar[4]).astype(F32)
    ones = jnp.ones((8, LANES), F32)
    scale_d = 1.0 / (ones * cfar[3].astype(F32))
    scale_d = jnp.concatenate([scale_d, scale_d], axis=0)
    scale_a = 1.0 / (ones * cfar[5].astype(F32))
    scale_a = jnp.concatenate([scale_a, scale_a], axis=0)
    doppler = (dop_far[...].astype(F32) + near_d * dop_near[...].astype(F32)).astype(BF16)

    lanes = lax.broadcasted_iota(jnp.int32, (8, LANES), 1)
    window = REACH_R - 1
    lead_in = jnp.clip(lanes - 1, 0, window).astype(F32)
    lag_in = jnp.clip(LANES - 2 - lanes, 0, window).astype(F32)
    lead_out, lag_out = window - lead_in, window - lag_in

    def weight_of(row, b):
        return blank[physical(row), b].astype(F32)

    @pl.loop(0, ROWS)
    def _(row):
        weights = [weight_of(row, b) for b in range(BLOCKS)]
        for b in range(BLOCKS):
            lead, lag = weights[b] * lead_in, weights[b] * lag_in
            if b > 0:
                lead = lead + weights[b - 1] * lead_out
            if b < BLOCKS - 1:
                lag = lag + weights[b + 1] * lag_out
            inverse[0, b, row] = 1.0 / jnp.maximum(lead, 1.0)
            inverse[1, b, row] = 1.0 / jnp.maximum(lag, 1.0)

    for edge in (0, BLOCKS + 1):
        weighted[edge] = jnp.zeros((ROWS, BINS, LANES), BF16)

    def integrate(rows, put):
        held_rows = [rows(e) for e in range(4)]
        last = None
        for t in range(put.count):
            held_rows.append(rows(t + 4))
            total = beams[0] * held_rows[0]
            for j in range(1, 5):
                total = total + beams[j] * held_rows[j]
            put(t, jnp.log(total + 0.05))
            held_rows.pop(0)

    def level_block(b):
        def rows(e):
            if e < HALO:
                return off[b, HALO - 1 - e].astype(F32)
            if e < HALO + ROWS:
                return power[0, b, e - HALO].astype(F32)
            return on[b, 2 * HALO + ROWS - 1 - e].astype(F32)

        def put(t, value):
            logs[t] = value
            row = t - REACH_A
            if 0 <= row < ROWS:
                rounded = value.astype(BF16)
                center[b, row] = rounded
                weighted[b + 1, row] = (
                    rounded.astype(F32) * weight_of(row, b)
                ).astype(BF16)

        put.count = SPAN
        integrate(rows, put)

        def edge_rows(e):
            if e < 2:
                return off_edge[b, 1 - e].astype(F32)
            if e < 2 + ROWS:
                return power[1, b, e - 2, 0:EDGE].astype(F32)
            return on_edge[b, 1 - (e - 2 - ROWS)].astype(F32)

        waiting = []

        def put_edge(t, value):
            waiting.append(value)
            if t % 2 == 1:
                logs_edge[t // 2] = jnp.concatenate(waiting, axis=0).astype(BF16)
                waiting.clear()

        put_edge.count = ROWS
        integrate(edge_rows, put_edge)

        means = []
        for group in range(ROWS // GROUP):
            stacked = jnp.concatenate(
                [
                    center[b, group * GROUP : (group + 1) * GROUP].reshape(
                        GROUP * BINS, LANES
                    ),
                    logs_edge[group * GROUP // 2 : (group + 1) * GROUP // 2].reshape(
                        GROUP * EDGE, LANES
                    ),
                ],
                axis=0,
            )
            sums = jnp.dot(doppler, stacked, preferred_element_type=F32)
            size = GROUP * BINS
            means.append(jnp.maximum(sums[:size], sums[size:]))

        far = REACH_A - 2
        lead = logs[0]
        lag = logs[REACH_A + 3]
        for d in range(1, far):
            lead = lead + logs[d]
            lag = lag + logs[REACH_A + 3 + d]
        for row in range(ROWS):
            azimuth = jnp.maximum(
                lead + near_a * logs[row + far], lag + near_a * logs[row + REACH_A + 2]
            )
            local = row % GROUP
            mean = means[row // GROUP][local * BINS : (local + 1) * BINS]
            level[b, row] = jnp.maximum(azimuth * scale_a, mean * scale_d)
            if row < ROWS - 1:
                lead = lead + (logs[row + far] - logs[row])
                lag = lag + (logs[row + REACH_A + 3 + far] - logs[row + REACH_A + 3])

    low = lax.broadcasted_iota(jnp.int32, (8, LANES), 0) < 4

    def emit(b):
        cells = pl.ds(pl.multiple_of(b * LANES, LANES), LANES)
        return pltpu.make_async_copy(out.at[b], result.at[:, :, cells], out_sem.at[b])

    def finish_block(b):
        stacked = jnp.concatenate(
            [weighted[b + i].reshape(ROWS * BINS, LANES) for i in range(3)], axis=1
        )
        sums = jnp.dot(stacked, band[...], preferred_element_type=F32)
        for row in range(ROWS):
            here = slice(row * BINS, (row + 1) * BINS)
            lead, lag = inverse[0, b, row], inverse[1, b, row]
            lead = sums[here, :LANES] * jnp.concatenate([lead, lead], axis=0)
            lag = sums[here, LANES:] * jnp.concatenate([lag, lag], axis=0)
            noise = jnp.maximum(jnp.maximum(lead, lag), level[b, row])
            excess = weight_of(row, b) * (center[b, row].astype(F32) - noise)
            first, second = excess[:8], pltpu.roll(excess[8:], 4, 0)
            ordered = jnp.concatenate(
                [jnp.where(low, first, second), jnp.where(low, second, first)], axis=0
            )
            out[b, physical(row)] = ordered.astype(BF16)
        emit(b).start()

    def blocks_of(first, size, body):
        @pl.loop(0, 2 * size)
        def _(index):
            body(lax.div(index, size) * OWN + first + lax.rem(index, size))

    def process(c):
        for kind in (2, 3, 4, 5, 6, 7, 8, 9):
            receive(c, kind)
        blocks_of(c * PER, PER, level_block)
        if c == 0:
            finish_block(0)
        elif c < CHUNKS - 1:
            blocks_of(c * PER - 1, PER, finish_block)
        else:
            blocks_of(c * PER - 1, PER + 1, finish_block)
            finish_block(OWN)

    for c in range(CHUNKS):
        receive(c, 0)
        receive(c, 1)
        for kind in (6, 7, 8, 9):
            send(c, kind)
        if c > 0:
            process(c - 1)
    process(CHUNKS - 1)

    for copy in sent:
        copy.wait_send()

    @pl.loop(0, BLOCKS)
    def _(b):
        emit(b).wait()


def local(echoes, pulse_taper, beam_weights, blanking, cfar_sizes):
    far, near = doppler_bands(GROUP)
    hbm = pl.BlockSpec(memory_space=pltpu.HBM)
    return pl.pallas_call(
        kernel,
        out_shape=jax.ShapeDtypeStruct((ROWS, BINS, BLOCKS * LANES), BF16),
        in_specs=[hbm] * 9,
        out_specs=pl.BlockSpec(memory_space=pl.ANY),
        scratch_shapes=[
            pltpu.VMEM((1, PULSES), F32),
            pltpu.VMEM((2 * PULSES, 2 * PULSES), F32),
            pltpu.VMEM((3 * LANES, 2 * LANES), BF16),
            pltpu.VMEM((2 * GROUP * BINS, GROUP * (BINS + EDGE)), BF16),
            pltpu.VMEM((2 * GROUP * BINS, GROUP * (BINS + EDGE)), BF16),
            pltpu.SMEM((5,), F32),
            pltpu.SMEM((ROWS, BLOCKS), jnp.int32),
            pltpu.SMEM((6,), jnp.int32),
            pltpu.SemaphoreType.DMA((8,)),
            pltpu.VMEM((BLOCKS, ROWS, BINS, LANES), BF16),
            pltpu.VMEM((CHUNKS, 2, ROWS, PULSES, WIDE), BF16),
            pltpu.VMEM((2, BLOCKS, ROWS, BINS, LANES), BF16),
            pltpu.VMEM((BLOCKS, HALO, BINS, LANES), BF16),
            pltpu.VMEM((BLOCKS, 2, EDGE, LANES), BF16),
            pltpu.VMEM((BLOCKS, HALO, BINS, LANES), BF16),
            pltpu.VMEM((BLOCKS, 2, EDGE, LANES), BF16),
            pltpu.VMEM((SPAN, BINS, LANES), F32),
            pltpu.VMEM((ROWS // 2, BINS, LANES), BF16),
            pltpu.VMEM((BLOCKS, ROWS, BINS, LANES), BF16),
            pltpu.VMEM((BLOCKS + 2, ROWS, BINS, LANES), BF16),
            pltpu.VMEM((BLOCKS, ROWS, BINS, LANES), F32),
            pltpu.VMEM((2, BLOCKS, ROWS, 8, LANES), F32),
            pltpu.SemaphoreType.DMA((CHUNKS,)),
            pltpu.SemaphoreType.DMA((CHUNKS, KINDS)),
            pltpu.SemaphoreType.DMA((CHUNKS, KINDS)),
            pltpu.SemaphoreType.DMA((BLOCKS,)),
        ],
        compiler_params=pltpu.CompilerParams(
            collective_id=0, has_side_effects=True, vmem_limit_bytes=67043328
        ),
    )(
        echoes,
        pulse_taper.reshape(1, PULSES),
        jnp.asarray(trig_table()),
        jnp.asarray(range_band(), BF16),
        jnp.asarray(far, BF16),
        jnp.asarray(near, BF16),
        beam_weights,
        blanking,
        cfar_sizes,
    )


def solution(mesh):
    in_specs = (P(None, "az", None, "rd"), P(), P(), P("az", None), P())
    out_specs = P("az", "rd", None)
    return jax.shard_map(local, mesh=mesh, in_specs=in_specs, out_specs=out_specs, check_vma=False)
```

```python
import math

import jax
import jax.numpy as jnp
import numpy as np
from jax import lax
from jax.experimental import pallas as pl
from jax.experimental.pallas import tpu as pltpu
from jax.sharding import PartitionSpec as P

F32 = jnp.float32
BF16 = jnp.bfloat16
PULSES = 32
ROWS = 16
BINS = 16
LANES = 128
BLOCKS = 16
OWN = 8
CHUNKS = 4
PER = OWN // CHUNKS
WIDE = PER * LANES
REACH_R = 24
REACH_D = 4
REACH_A = 12
HALO = REACH_A + 2
SPAN = ROWS + 2 * REACH_A
ORDER = (0, 1, 2, 3, 12, 13, 14, 15, 4, 5, 6, 7, 8, 9, 10, 11)
EDGE = 8
PIECES = ((0, 2), (2, 2), (4, 2), (6, 1), (7, 1))
PAIR_KINDS, KINDS = 5, 13


def trig_table():
    bins = np.array([half * BINS + place for half in range(2) for place in ORDER])
    theta = 2.0 * np.pi * (np.outer(bins, np.arange(PULSES)) % PULSES) / PULSES
    cosines, sines = np.cos(theta), np.sin(theta)
    real = np.concatenate([cosines, sines], axis=1)
    imag = np.concatenate([-sines, cosines], axis=1)
    return np.concatenate([real, imag], axis=0).astype(np.float32)


def range_band():
    source = np.arange(3 * LANES)[:, None] - LANES
    lane = np.arange(LANES)[None, :]
    lead, lag = lane - source, source - lane
    bands = [((d > 1) & (d <= REACH_R)) for d in (lead, lag)]
    return np.concatenate(bands, axis=1).astype(np.float32)


def doppler_bands(group):
    tables = []
    for offsets in ((3, 4), (2,)):
        table = np.zeros((2, group, BINS, group * (BINS + EDGE)), np.float32)
        for side, sign in enumerate((-1, 1)):
            for row in range(group):
                for slot, place in enumerate(ORDER):
                    for offset in offsets:
                        source = (place + sign * offset) % PULSES
                        spot = ORDER.index(source % BINS)
                        if source < BINS:
                            column = row * BINS + spot
                        else:
                            column = group * BINS + row * EDGE + spot
                        table[side, row, slot, column] += 1.0
        tables.append(table.reshape(2 * group * BINS, -1))
    return tables


GROUP = 8


def kernel(
    echoes,
    *refs,
):
    sources, (result, *scratch) = refs[:8], refs[8:]
    tables, (stage_sem, *scratch) = scratch[:8], scratch[8:]
    stages = []
    for index, (source, table) in enumerate(zip(sources, tables)):
        stage = pltpu.make_async_copy(source, table, stage_sem.at[index])
        stages.append(stage)
    body(echoes, result, stages, *tables, *scratch)


def body(
    echoes,
    result,
    stages,
    taper,
    trig,
    band,
    dop_far,
    dop_near,
    beam,
    blank,
    cfar,
    out,
    held,
    power,
    off,
    off_edge,
    on,
    on_edge,
    logs,
    logs_edge,
    center,
    weighted,
    level,
    inverse,
    load_sem,
    send_sem,
    recv_sem,
    out_sem,
):
    az, rd = lax.axis_index("az"), lax.axis_index("rd")
    count = lax.axis_size("az")
    odd = lax.rem(az, 2)
    pair = (az, 1 - rd)
    outer = (lax.rem(az - 1 + 2 * odd + count, count), 1 - rd)
    inner = (az + 1 - 2 * odd, rd)

    def physical(row):
        return row + odd * (ROWS - 1 - 2 * row)

    def block_at(half, place):
        return OWN - 1 - place + half * (1 + 2 * place)

    loads = []
    for c in range(CHUNKS):
        first = (rd * c + (1 - rd) * (CHUNKS - 1 - c)) * WIDE
        load = pltpu.make_async_copy(
            echoes.at[:, :, :, pl.ds(pl.multiple_of(first, WIDE), WIDE)],
            held.at[c],
            load_sem.at[c],
        )
        loads.append(load)
    for stage in stages[:2]:
        stage.start()
    for load in loads:
        load.start()
    for stage in stages[2:]:
        stage.start()

    barrier = pltpu.get_barrier_semaphore()
    for target in (pair, outer, inner):
        pl.semaphore_signal(
            barrier, inc=1, device_id=target, device_id_type=pl.DeviceIdType.MESH
        )

    def transfer(c, kind, half):
        place, size = PIECES[c]
        blocks = pl.ds(half * OWN + place, size)
        what = kind if kind < PAIR_KINDS + 4 else kind - 4
        if what < PAIR_KINDS:
            bins, cut = (
                (0, (pl.ds(0, HALO),)),
                (0, (pl.ds(HALO, 2), pl.ds(0, EDGE))),
                (1, (pl.ds(0, 2), pl.ds(0, EDGE))),
                (1, (pl.ds(2, HALO),)),
                (1, (pl.ds(0, 2), pl.ds(EDGE, EDGE))),
            )[what]
            src = power.at[(bins, blocks) + cut]
            dst, target = power.at[(1 - bins, blocks) + cut], pair
        elif what == 5:
            src, dst, target = power.at[1, blocks, pl.ds(0, HALO)], off.at[blocks], outer
        elif what == 6:
            src = power.at[0, blocks, pl.ds(0, 2), pl.ds(0, EDGE)]
            dst, target = off_edge.at[blocks], outer
        elif what == 7:
            src = power.at[0, blocks, pl.ds(ROWS - HALO, HALO)]
            dst, target = on.at[blocks], inner
        else:
            src = power.at[1, blocks, pl.ds(ROWS - 2, 2), pl.ds(0, EDGE)]
            dst, target = on_edge.at[blocks], inner
        return pltpu.make_async_remote_copy(
            src_ref=src,
            dst_ref=dst,
            send_sem=send_sem.at[c, kind],
            recv_sem=recv_sem.at[c, kind],
            device_id=target,
            device_id_type=pl.DeviceIdType.MESH,
        )

    sent = []

    def send(c, *kinds):
        for kind in kinds:
            copy = transfer(c, kind, rd if kind < PAIR_KINDS + 4 else 1 - rd)
            copy.start()
            sent.append(copy)

    def receive(c, *kinds):
        for kind in kinds:
            other = kind < PAIR_KINDS + 2 or kind > PAIR_KINDS + 5
            transfer(c, kind, 1 - rd if other else rd).wait_recv()

    for stage in stages[:2]:
        stage.wait()
    lane_parity = lax.rem(lax.broadcasted_iota(jnp.int32, (1, PULSES), 1), 2)
    signs = 1.0 - (2 * rd * lane_parity).astype(F32)
    tapered = taper[...] * signs
    bank = (trig[...] * jnp.concatenate([tapered, tapered], axis=1)).astype(BF16)

    for c in range(CHUNKS):
        loads[c].wait()
        for row in range(ROWS):
            spot = physical(row)
            pulses = jnp.concatenate([held[c, 0, spot], held[c, 1, spot]], axis=0)
            spectrum = jnp.dot(bank, pulses, preferred_element_type=F32)
            real, imag = spectrum[:PULSES], spectrum[PULSES:]
            powers = (real * real + imag * imag).astype(BF16)
            for part in range(PER):
                place = c * PER + part * rd + (PER - 1 - part) * (1 - rd)
                for half in range(2):
                    power[half, rd * OWN + place, row] = powers[
                        half * BINS : (half + 1) * BINS, part * LANES : (part + 1) * LANES
                    ]
        if c == 0:
            pl.semaphore_wait(barrier, 3)
        for piece, (place, _) in enumerate(PIECES):
            if place // PER == c:
                send(piece, 0, 1, 2, 5, 6, 7, 8)
    for piece in range(len(PIECES)):
        send(piece, 3, 4)

    for stage in stages[2:]:
        stage.wait()
    beams = [
        (beam[j] + odd.astype(F32) * (beam[4 - j] - beam[j])) * (1.0 / PULSES)
        for j in range(5)
    ]
    near_d = (2 - cfar[2]).astype(F32)
    near_a = (2 - cfar[4]).astype(F32)
    ones = jnp.ones((8, LANES), F32)
    scale_d = 1.0 / (ones * cfar[3].astype(F32))
    scale_d = jnp.concatenate([scale_d, scale_d], axis=0)
    scale_a = 1.0 / (ones * cfar[5].astype(F32))
    scale_a = jnp.concatenate([scale_a, scale_a], axis=0)
    doppler = (dop_far[...].astype(F32) + near_d * dop_near[...].astype(F32)).astype(BF16)

    lanes = lax.broadcasted_iota(jnp.int32, (8, LANES), 1)
    window = REACH_R - 1
    lead_in = jnp.clip(lanes - 1, 0, window).astype(F32)
    lag_in = jnp.clip(LANES - 2 - lanes, 0, window).astype(F32)
    lead_out, lag_out = window - lead_in, window - lag_in

    def weight_of(row, b):
        return blank[physical(row), b].astype(F32)

    @pl.loop(0, ROWS)
    def _(row):
        weights = [weight_of(row, b) for b in range(BLOCKS)]
        for b in range(BLOCKS):
            lead, lag = weights[b] * lead_in, weights[b] * lag_in
            if b > 0:
                lead = lead + weights[b - 1] * lead_out
            if b < BLOCKS - 1:
                lag = lag + weights[b + 1] * lag_out
            inverse[0, b, row] = 1.0 / jnp.maximum(lead, 1.0)
            inverse[1, b, row] = 1.0 / jnp.maximum(lag, 1.0)

    for edge in (0, BLOCKS + 1):
        weighted[edge] = jnp.zeros((ROWS, BINS, LANES), BF16)

    def integrate(rows, put):
        held_rows = [rows(e) for e in range(4)]
        last = None
        for t in range(put.count):
            held_rows.append(rows(t + 4))
            total = beams[0] * held_rows[0]
            for j in range(1, 5):
                total = total + beams[j] * held_rows[j]
            put(t, jnp.log(total + 0.05))
            held_rows.pop(0)

    def level_block(half, place):
        b, q = block_at(half, place), half * OWN + place

        def rows(e):
            if e < HALO:
                return off[q, HALO - 1 - e].astype(F32)
            if e < HALO + ROWS:
                return power[0, q, e - HALO].astype(F32)
            return on[q, 2 * HALO + ROWS - 1 - e].astype(F32)

        def put(t, value):
            logs[t] = value
            row = t - REACH_A
            if 0 <= row < ROWS:
                rounded = value.astype(BF16)
                center[b, row] = rounded
                weighted[b + 1, row] = (
                    rounded.astype(F32) * weight_of(row, b)
                ).astype(BF16)

        put.count = SPAN
        integrate(rows, put)

        def edge_rows(e):
            if e < 2:
                return off_edge[q, 1 - e].astype(F32)
            if e < 2 + ROWS:
                return power[1, q, e - 2, 0:EDGE].astype(F32)
            return on_edge[q, 1 - (e - 2 - ROWS)].astype(F32)

        waiting = []

        def put_edge(t, value):
            waiting.append(value)
            if t % 2 == 1:
                logs_edge[t // 2] = jnp.concatenate(waiting, axis=0).astype(BF16)
                waiting.clear()

        put_edge.count = ROWS
        integrate(edge_rows, put_edge)

        means = []
        for group in range(ROWS // GROUP):
            stacked = jnp.concatenate(
                [
                    center[b, group * GROUP : (group + 1) * GROUP].reshape(
                        GROUP * BINS, LANES
                    ),
                    logs_edge[group * GROUP // 2 : (group + 1) * GROUP // 2].reshape(
                        GROUP * EDGE, LANES
                    ),
                ],
                axis=0,
            )
            sums = jnp.dot(doppler, stacked, preferred_element_type=F32)
            size = GROUP * BINS
            means.append(jnp.maximum(sums[:size], sums[size:]))

        far = REACH_A - 2
        lead = logs[0]
        lag = logs[REACH_A + 3]
        for d in range(1, far):
            lead = lead + logs[d]
            lag = lag + logs[REACH_A + 3 + d]
        for row in range(ROWS):
            azimuth = jnp.maximum(
                lead + near_a * logs[row + far], lag + near_a * logs[row + REACH_A + 2]
            )
            local = row % GROUP
            mean = means[row // GROUP][local * BINS : (local + 1) * BINS]
            level[b, row] = jnp.maximum(azimuth * scale_a, mean * scale_d)
            if row < ROWS - 1:
                lead = lead + (logs[row + far] - logs[row])
                lag = lag + (logs[row + REACH_A + 3 + far] - logs[row + REACH_A + 3])

    low = lax.broadcasted_iota(jnp.int32, (8, LANES), 0) < 4

    def emit(b):
        cells = pl.ds(pl.multiple_of(b * LANES, LANES), LANES)
        return pltpu.make_async_copy(out.at[b], result.at[:, :, cells], out_sem.at[b])

    def finish_block(b):
        stacked = jnp.concatenate(
            [weighted[b + i].reshape(ROWS * BINS, LANES) for i in range(3)], axis=1
        )
        sums = jnp.dot(stacked, band[...], preferred_element_type=F32)
        for row in range(ROWS):
            here = slice(row * BINS, (row + 1) * BINS)
            lead, lag = inverse[0, b, row], inverse[1, b, row]
            lead = sums[here, :LANES] * jnp.concatenate([lead, lead], axis=0)
            lag = sums[here, LANES:] * jnp.concatenate([lag, lag], axis=0)
            noise = jnp.maximum(jnp.maximum(lead, lag), level[b, row])
            excess = weight_of(row, b) * (center[b, row].astype(F32) - noise)
            first, second = excess[:8], pltpu.roll(excess[8:], 4, 0)
            ordered = jnp.concatenate(
                [jnp.where(low, first, second), jnp.where(low, second, first)], axis=0
            )
            out[b, physical(row)] = ordered.astype(BF16)
        emit(b).start()

    def levels(c, half):
        place, size = PIECES[c]

        @pl.loop(0, size)
        def _(index):
            level_block(half, place + index)

    def finishes(first, size):
        @pl.loop(0, 2 * size)
        def _(index):
            finish_block(block_at(lax.div(index, size), first + lax.rem(index, size)))

    for c in range(len(PIECES)):
        receive(c, 0, 1, 2)
        send(c, 9, 10)
    for c, (place, size) in enumerate(PIECES):
        receive(c, 3, 4)
        send(c, 11, 12)
        receive(c, 9, 10, 7, 8)
        levels(c, rd)
        receive(c, 11, 12, 5, 6)
        levels(c, 1 - rd)
        first = max(place - 1, 0)
        last = place + size - (c < len(PIECES) - 1)
        finishes(first, last - first)

    for copy in sent:
        copy.wait_send()

    @pl.loop(0, BLOCKS)
    def _(b):
        emit(b).wait()


def local(echoes, pulse_taper, beam_weights, blanking, cfar_sizes):
    far, near = doppler_bands(GROUP)
    hbm = pl.BlockSpec(memory_space=pltpu.HBM)
    return pl.pallas_call(
        kernel,
        out_shape=jax.ShapeDtypeStruct((ROWS, BINS, BLOCKS * LANES), BF16),
        in_specs=[hbm] * 9,
        out_specs=pl.BlockSpec(memory_space=pl.ANY),
        scratch_shapes=[
            pltpu.VMEM((1, PULSES), F32),
            pltpu.VMEM((2 * PULSES, 2 * PULSES), F32),
            pltpu.VMEM((3 * LANES, 2 * LANES), BF16),
            pltpu.VMEM((2 * GROUP * BINS, GROUP * (BINS + EDGE)), BF16),
            pltpu.VMEM((2 * GROUP * BINS, GROUP * (BINS + EDGE)), BF16),
            pltpu.SMEM((5,), F32),
            pltpu.SMEM((ROWS, BLOCKS), jnp.int32),
            pltpu.SMEM((6,), jnp.int32),
            pltpu.SemaphoreType.DMA((8,)),
            pltpu.VMEM((BLOCKS, ROWS, BINS, LANES), BF16),
            pltpu.VMEM((CHUNKS, 2, ROWS, PULSES, WIDE), BF16),
            pltpu.VMEM((2, BLOCKS, ROWS, BINS, LANES), BF16),
            pltpu.VMEM((BLOCKS, HALO, BINS, LANES), BF16),
            pltpu.VMEM((BLOCKS, 2, EDGE, LANES), BF16),
            pltpu.VMEM((BLOCKS, HALO, BINS, LANES), BF16),
            pltpu.VMEM((BLOCKS, 2, EDGE, LANES), BF16),
            pltpu.VMEM((SPAN, BINS, LANES), F32),
            pltpu.VMEM((ROWS // 2, BINS, LANES), BF16),
            pltpu.VMEM((BLOCKS, ROWS, BINS, LANES), BF16),
            pltpu.VMEM((BLOCKS + 2, ROWS, BINS, LANES), BF16),
            pltpu.VMEM((BLOCKS, ROWS, BINS, LANES), F32),
            pltpu.VMEM((2, BLOCKS, ROWS, 8, LANES), F32),
            pltpu.SemaphoreType.DMA((CHUNKS,)),
            pltpu.SemaphoreType.DMA((len(PIECES), KINDS)),
            pltpu.SemaphoreType.DMA((len(PIECES), KINDS)),
            pltpu.SemaphoreType.DMA((BLOCKS,)),
        ],
        compiler_params=pltpu.CompilerParams(
            collective_id=0, has_side_effects=True, vmem_limit_bytes=48<<20
        ),
    )(
        *(pltpu.with_memory_space_constraint(x, pltpu.HBM) for x in (
        echoes,
        pulse_taper.reshape(1, PULSES),
        jnp.asarray(trig_table()),
        jnp.asarray(range_band(), BF16),
        jnp.asarray(far, BF16),
        jnp.asarray(near, BF16),
        beam_weights,
        blanking,
        cfar_sizes,
        ))
    )


def solution(mesh):
    in_specs = (P(None, "az", None, "rd"), P(), P(), P("az", None), P())
    out_specs = P("az", "rd", None)
    return jax.shard_map(local, mesh=mesh, in_specs=in_specs, out_specs=out_specs, check_vma=False)
```

```python
import math

import jax
import jax.numpy as jnp
import numpy as np
from jax import lax
from jax.experimental import pallas as pl
from jax.experimental.pallas import tpu as pltpu
from jax.sharding import PartitionSpec as P

F32 = jnp.float32
BF16 = jnp.bfloat16
PULSES = 32
ROWS = 16
BINS = 16
LANES = 128
BLOCKS = 16
OWN = 8
CHUNKS = 4
PER = OWN // CHUNKS
WIDE = PER * LANES
REACH_R = 24
REACH_D = 4
REACH_A = 12
HALO = REACH_A + 2
SPAN = ROWS + 2 * REACH_A
ORDER = (0, 1, 2, 3, 12, 13, 14, 15, 4, 5, 6, 7, 8, 9, 10, 11)
EDGE = 8
PIECES = ((0, 2), (2, 2), (4, 2), (6, 1), (7, 1))
AHEAD = 2
PAIR_KINDS, KINDS = 5, 13


def trig_table():
    bins = np.array([half * BINS + place for half in range(2) for place in ORDER])
    theta = 2.0 * np.pi * (np.outer(bins, np.arange(PULSES)) % PULSES) / PULSES
    cosines, sines = np.cos(theta), np.sin(theta)
    real = np.concatenate([cosines, sines], axis=1)
    imag = np.concatenate([-sines, cosines], axis=1)
    return np.concatenate([real, imag], axis=0).astype(np.float32)


def range_band():
    source = np.arange(3 * LANES)[:, None] - LANES
    lane = np.arange(LANES)[None, :]
    lead, lag = lane - source, source - lane
    bands = [((d > 1) & (d <= REACH_R)) for d in (lead, lag)]
    return np.concatenate(bands, axis=1).astype(np.float32)


def doppler_bands(group):
    tables = []
    for offsets in ((3, 4), (2,)):
        table = np.zeros((2, group, BINS, group * (BINS + EDGE)), np.float32)
        for side, sign in enumerate((-1, 1)):
            for row in range(group):
                for slot, place in enumerate(ORDER):
                    for offset in offsets:
                        source = (place + sign * offset) % PULSES
                        spot = ORDER.index(source % BINS)
                        if source < BINS:
                            column = row * BINS + spot
                        else:
                            column = group * BINS + row * EDGE + spot
                        table[side, row, slot, column] += 1.0
        tables.append(table.reshape(2 * group * BINS, -1))
    return tables


GROUP = 8


def kernel(
    echoes,
    *refs,
):
    sources, (result, *scratch) = refs[:8], refs[8:]
    tables, (stage_sem, *scratch) = scratch[:8], scratch[8:]
    stages = []
    for index, (source, table) in enumerate(zip(sources, tables)):
        stage = pltpu.make_async_copy(source, table, stage_sem.at[index])
        stages.append(stage)
    body(echoes, result, stages, *tables, *scratch)


def body(
    echoes,
    result,
    stages,
    taper,
    trig,
    band,
    dop_far,
    dop_near,
    beam,
    blank,
    cfar,
    held,
    power,
    off,
    off_edge,
    on,
    on_edge,
    logs,
    logs_edge,
    center,
    weighted,
    level,
    inverse,
    load_sem,
    send_sem,
    recv_sem,
):
    az, rd = lax.axis_index("az"), lax.axis_index("rd")
    count = lax.axis_size("az")
    odd = lax.rem(az, 2)
    pair = (az, 1 - rd)
    outer = (lax.rem(az - 1 + 2 * odd + count, count), 1 - rd)
    inner = (az + 1 - 2 * odd, rd)

    def physical(row):
        return row + odd * (ROWS - 1 - 2 * row)

    def block_at(half, place):
        return OWN - 1 - place + half * (1 + 2 * place)

    loads = []
    for c in range(CHUNKS):
        first = (rd * c + (1 - rd) * (CHUNKS - 1 - c)) * WIDE
        load = pltpu.make_async_copy(
            echoes.at[:, :, :, pl.ds(pl.multiple_of(first, WIDE), WIDE)],
            held.at[c],
            load_sem.at[c],
        )
        loads.append(load)
    for stage in stages[:2]:
        stage.start()
    for load in loads:
        load.start()
    for stage in stages[2:]:
        stage.start()

    barrier = pltpu.get_barrier_semaphore()
    for target in (pair, outer, inner):
        pl.semaphore_signal(
            barrier, inc=1, device_id=target, device_id_type=pl.DeviceIdType.MESH
        )

    def transfer(c, kind, half):
        place, size = PIECES[c]
        blocks = pl.ds(half * OWN + place, size)
        what = kind if kind < PAIR_KINDS + 4 else kind - 4
        if what < PAIR_KINDS:
            bins, cut = (
                (0, (pl.ds(0, HALO),)),
                (0, (pl.ds(HALO, 2), pl.ds(0, EDGE))),
                (1, (pl.ds(0, 2), pl.ds(0, EDGE))),
                (1, (pl.ds(2, HALO),)),
                (1, (pl.ds(0, 2), pl.ds(EDGE, EDGE))),
            )[what]
            src = power.at[(bins, blocks) + cut]
            dst, target = power.at[(1 - bins, blocks) + cut], pair
        elif what == 5:
            src, dst, target = power.at[1, blocks, pl.ds(0, HALO)], off.at[blocks], outer
        elif what == 6:
            src = power.at[0, blocks, pl.ds(0, 2), pl.ds(0, EDGE)]
            dst, target = off_edge.at[blocks], outer
        elif what == 7:
            src = power.at[0, blocks, pl.ds(ROWS - HALO, HALO)]
            dst, target = on.at[blocks], inner
        else:
            src = power.at[1, blocks, pl.ds(ROWS - 2, 2), pl.ds(0, EDGE)]
            dst, target = on_edge.at[blocks], inner
        return pltpu.make_async_remote_copy(
            src_ref=src,
            dst_ref=dst,
            send_sem=send_sem.at[c, kind],
            recv_sem=recv_sem.at[c, kind],
            device_id=target,
            device_id_type=pl.DeviceIdType.MESH,
        )

    urgent = az == count - 1

    def send(c, *kinds):
        for kind in kinds:
            transfer(c, kind, rd if kind < PAIR_KINDS + 4 else 1 - rd).start()

    def receive(c, *kinds):
        for kind in kinds:
            other = kind < PAIR_KINDS + 2 or kind > PAIR_KINDS + 5
            transfer(c, kind, 1 - rd if other else rd).wait_recv()

    for stage in stages[:2]:
        stage.wait()
    lane_parity = lax.rem(lax.broadcasted_iota(jnp.int32, (1, PULSES), 1), 2)
    signs = 1.0 - (2 * rd * lane_parity).astype(F32)
    tapered = taper[...] * signs
    bank = (trig[...] * jnp.concatenate([tapered, tapered], axis=1)).astype(BF16)

    for c in range(CHUNKS):
        loads[c].wait()
        for row in range(ROWS):
            spot = physical(row)
            pulses = jnp.concatenate([held[c, 0, spot], held[c, 1, spot]], axis=0)
            spectrum = jnp.dot(bank, pulses, preferred_element_type=F32)
            real, imag = spectrum[:PULSES], spectrum[PULSES:]
            powers = (real * real + imag * imag).astype(BF16)
            for part in range(PER):
                place = c * PER + part * rd + (PER - 1 - part) * (1 - rd)
                for half in range(2):
                    power[half, rd * OWN + place, row] = powers[
                        half * BINS : (half + 1) * BINS, part * LANES : (part + 1) * LANES
                    ]
        if c == 0:
            pl.semaphore_wait(barrier, 3)
        for piece, (place, _) in enumerate(PIECES):
            if place // PER == c:
                send(piece, 0, 1, 2, 7, 8)

                if piece < AHEAD:
                    send(piece, 5, 6)
                else:

                    @pl.when(urgent)
                    def _():
                        send(piece, 5, 6)

                if piece > 0:

                    @pl.when(jnp.logical_not(urgent))
                    def _():
                        send(piece - 1, 3, 4)

    @pl.when(jnp.logical_not(urgent))
    def _():
        send(len(PIECES) - 1, 3, 4)

    @pl.when(urgent)
    def _():
        for piece in range(len(PIECES)):
            send(piece, 3, 4)


    for stage in stages[2:]:
        stage.wait()
    beams = [
        (beam[j] + odd.astype(F32) * (beam[4 - j] - beam[j])) * (1.0 / PULSES)
        for j in range(5)
    ]
    near_d = (2 - cfar[2]).astype(F32)
    near_a = (2 - cfar[4]).astype(F32)
    ones = jnp.ones((8, LANES), F32)
    scale_d = 1.0 / (ones * cfar[3].astype(F32))
    scale_d = jnp.concatenate([scale_d, scale_d], axis=0)
    scale_a = 1.0 / (ones * cfar[5].astype(F32))
    scale_a = jnp.concatenate([scale_a, scale_a], axis=0)
    doppler = (dop_far[...].astype(F32) + near_d * dop_near[...].astype(F32)).astype(BF16)

    lanes = lax.broadcasted_iota(jnp.int32, (8, LANES), 1)
    window = REACH_R - 1
    lead_in = jnp.clip(lanes - 1, 0, window).astype(F32)
    lag_in = jnp.clip(LANES - 2 - lanes, 0, window).astype(F32)
    lead_out, lag_out = window - lead_in, window - lag_in

    def weight_of(row, b):
        return blank[physical(row), b].astype(F32)

    @pl.loop(0, ROWS)
    def _(row):
        weights = [weight_of(row, b) for b in range(BLOCKS)]
        for b in range(BLOCKS):
            lead, lag = weights[b] * lead_in, weights[b] * lag_in
            if b > 0:
                lead = lead + weights[b - 1] * lead_out
            if b < BLOCKS - 1:
                lag = lag + weights[b + 1] * lag_out
            inverse[0, b, row] = 1.0 / jnp.maximum(lead, 1.0)
            inverse[1, b, row] = 1.0 / jnp.maximum(lag, 1.0)

    for edge in (0, BLOCKS + 1):
        weighted[edge] = jnp.zeros((ROWS, BINS, LANES), BF16)

    def integrate(rows, put):
        held_rows = [rows(e) for e in range(4)]
        last = None
        for t in range(put.count):
            held_rows.append(rows(t + 4))
            total = beams[0] * held_rows[0]
            for j in range(1, 5):
                total = total + beams[j] * held_rows[j]
            put(t, jnp.log(total + 0.05))
            held_rows.pop(0)

    def level_block(half, place):
        b, q = block_at(half, place), half * OWN + place

        def rows(e):
            if e < HALO:
                return off[q, HALO - 1 - e].astype(F32)
            if e < HALO + ROWS:
                return power[0, q, e - HALO].astype(F32)
            return on[q, 2 * HALO + ROWS - 1 - e].astype(F32)

        def put(t, value):
            logs[t] = value
            row = t - REACH_A
            if 0 <= row < ROWS:
                rounded = value.astype(BF16)
                center[b, row] = rounded
                weighted[b + 1, row] = (
                    rounded.astype(F32) * weight_of(row, b)
                ).astype(BF16)

        put.count = SPAN
        integrate(rows, put)

        def edge_rows(e):
            if e < 2:
                return off_edge[q, 1 - e].astype(F32)
            if e < 2 + ROWS:
                return power[1, q, e - 2, 0:EDGE].astype(F32)
            return on_edge[q, 1 - (e - 2 - ROWS)].astype(F32)

        waiting = []

        def put_edge(t, value):
            waiting.append(value)
            if t % 2 == 1:
                logs_edge[t // 2] = jnp.concatenate(waiting, axis=0).astype(BF16)
                waiting.clear()

        put_edge.count = ROWS
        integrate(edge_rows, put_edge)

        means = []
        for group in range(ROWS // GROUP):
            stacked = jnp.concatenate(
                [
                    center[b, group * GROUP : (group + 1) * GROUP].reshape(
                        GROUP * BINS, LANES
                    ),
                    logs_edge[group * GROUP // 2 : (group + 1) * GROUP // 2].reshape(
                        GROUP * EDGE, LANES
                    ),
                ],
                axis=0,
            )
            sums = jnp.dot(doppler, stacked, preferred_element_type=F32)
            size = GROUP * BINS
            means.append(jnp.maximum(sums[:size], sums[size:]))

        far = REACH_A - 2
        lead = logs[0]
        lag = logs[REACH_A + 3]
        for d in range(1, far):
            lead = lead + logs[d]
            lag = lag + logs[REACH_A + 3 + d]
        for row in range(ROWS):
            azimuth = jnp.maximum(
                lead + near_a * logs[row + far], lag + near_a * logs[row + REACH_A + 2]
            )
            local = row % GROUP
            mean = means[row // GROUP][local * BINS : (local + 1) * BINS]
            level[b, row] = jnp.maximum(azimuth * scale_a, mean * scale_d)
            if row < ROWS - 1:
                lead = lead + (logs[row + far] - logs[row])
                lag = lag + (logs[row + REACH_A + 3 + far] - logs[row + REACH_A + 3])

    low = lax.broadcasted_iota(jnp.int32, (8, LANES), 0) < 4

    def finish_block(b):
        cells = pl.ds(pl.multiple_of(b * LANES, LANES), LANES)
        stacked = jnp.concatenate(
            [weighted[b + i].reshape(ROWS * BINS, LANES) for i in range(3)], axis=1
        )
        sums = jnp.dot(stacked, band[...], preferred_element_type=F32)
        for row in range(ROWS):
            here = slice(row * BINS, (row + 1) * BINS)
            lead, lag = inverse[0, b, row], inverse[1, b, row]
            lead = sums[here, :LANES] * jnp.concatenate([lead, lead], axis=0)
            lag = sums[here, LANES:] * jnp.concatenate([lag, lag], axis=0)
            noise = jnp.maximum(jnp.maximum(lead, lag), level[b, row])
            excess = weight_of(row, b) * (center[b, row].astype(F32) - noise)
            first, second = excess[:8], pltpu.roll(excess[8:], 4, 0)
            ordered = jnp.concatenate(
                [jnp.where(low, first, second), jnp.where(low, second, first)], axis=0
            )
            result[physical(row), :, cells] = ordered.astype(BF16)

    def levels(c, half):
        place, size = PIECES[c]

        @pl.loop(0, size)
        def _(index):
            level_block(half, place + index)

    def finishes(first, size):
        @pl.loop(0, size)
        def _(index):
            finish_block(block_at(0, first + index))
            finish_block(block_at(1, first + index))

    def relay(c):
        if c < len(PIECES):
            receive(c, 0, 1, 2)
            send(c, 9, 10)
        if c + AHEAD < len(PIECES):

            @pl.when(jnp.logical_not(urgent))
            def _():
                send(c + AHEAD, 5, 6)

    for c in range(AHEAD):
        relay(c)

    @pl.when(urgent)
    def _():
        for c in range(AHEAD, len(PIECES)):
            relay(c)

    for c, (place, size) in enumerate(PIECES):
        receive(c, 3, 4)
        send(c, 11, 12)
        receive(c, 9, 10, 7, 8)
        levels(c, rd)

        @pl.when(jnp.logical_not(urgent))
        def _():
            relay(c + AHEAD)

        receive(c, 11, 12, 5, 6)
        levels(c, 1 - rd)
        first = max(place - 1, 0)
        last = place + size - (c < len(PIECES) - 1)
        finishes(first, last - first)

    for c in range(len(PIECES)):
        for kind in range(KINDS):
            transfer(c, kind, rd if kind < PAIR_KINDS + 4 else 1 - rd).wait_send()


def local(echoes, pulse_taper, beam_weights, blanking, cfar_sizes):
    far, near = doppler_bands(GROUP)
    hbm = pl.BlockSpec(memory_space=pltpu.HBM)
    return pl.pallas_call(
        kernel,
        out_shape=jax.ShapeDtypeStruct((ROWS, BINS, BLOCKS * LANES), BF16),
        in_specs=[hbm] * 9,
        out_specs=pl.BlockSpec(memory_space=pltpu.VMEM),
        scratch_shapes=[
            pltpu.VMEM((1, PULSES), F32),
            pltpu.VMEM((2 * PULSES, 2 * PULSES), F32),
            pltpu.VMEM((3 * LANES, 2 * LANES), BF16),
            pltpu.VMEM((2 * GROUP * BINS, GROUP * (BINS + EDGE)), BF16),
            pltpu.VMEM((2 * GROUP * BINS, GROUP * (BINS + EDGE)), BF16),
            pltpu.SMEM((5,), F32),
            pltpu.SMEM((ROWS, BLOCKS), jnp.int32),
            pltpu.SMEM((6,), jnp.int32),
            pltpu.SemaphoreType.DMA((8,)),
            pltpu.VMEM((CHUNKS, 2, ROWS, PULSES, WIDE), BF16),
            pltpu.VMEM((2, BLOCKS, ROWS, BINS, LANES), BF16),
            pltpu.VMEM((BLOCKS, HALO, BINS, LANES), BF16),
            pltpu.VMEM((BLOCKS, 2, EDGE, LANES), BF16),
            pltpu.VMEM((BLOCKS, HALO, BINS, LANES), BF16),
            pltpu.VMEM((BLOCKS, 2, EDGE, LANES), BF16),
            pltpu.VMEM((SPAN, BINS, LANES), F32),
            pltpu.VMEM((ROWS // 2, BINS, LANES), BF16),
            pltpu.VMEM((BLOCKS, ROWS, BINS, LANES), BF16),
            pltpu.VMEM((BLOCKS + 2, ROWS, BINS, LANES), BF16),
            pltpu.VMEM((BLOCKS, ROWS, BINS, LANES), F32),
            pltpu.VMEM((2, BLOCKS, ROWS, 8, LANES), F32),
            pltpu.SemaphoreType.DMA((CHUNKS,)),
            pltpu.SemaphoreType.DMA((len(PIECES), KINDS)),
            pltpu.SemaphoreType.DMA((len(PIECES), KINDS)),
        ],
        compiler_params=pltpu.CompilerParams(
            collective_id=0, has_side_effects=True, vmem_limit_bytes=48<<20
        ),
    )(
        *(pltpu.with_memory_space_constraint(x, pltpu.HBM) for x in (
        echoes,
        pulse_taper.reshape(1, PULSES),
        jnp.asarray(trig_table()),
        jnp.asarray(range_band(), BF16),
        jnp.asarray(far, BF16),
        jnp.asarray(near, BF16),
        beam_weights,
        blanking,
        cfar_sizes,
        ))
    )


def solution(mesh):
    in_specs = (P(None, "az", None, "rd"), P(), P(), P("az", None), P())
    out_specs = P("az", "rd", None)
    return jax.shard_map(local, mesh=mesh, in_specs=in_specs, out_specs=out_specs, check_vma=False)
```

```python
import math

import jax
import jax.numpy as jnp
import numpy as np
from jax import lax
from jax.experimental import pallas as pl
from jax.experimental.pallas import tpu as pltpu
from jax.sharding import PartitionSpec as P

F32 = jnp.float32
BF16 = jnp.bfloat16
PULSES = 32
ROWS = 16
BINS = 16
LANES = 128
BLOCKS = 16
OWN = 8
CHUNKS = 4
PER = OWN // CHUNKS
WIDE = PER * LANES
REACH_R = 24
REACH_D = 4
REACH_A = 12
HALO = REACH_A + 2
SPAN = ROWS + 2 * REACH_A
ORDER = (0, 1, 2, 3, 12, 13, 14, 15, 4, 5, 6, 7, 8, 9, 10, 11)
EDGE = 8
PIECES = ((0, 2), (2, 2), (4, 2), (6, 1), (7, 1))
AHEAD = 2
PAIR_KINDS, KINDS = 5, 13


def trig_table():
    bins = np.array([half * BINS + place for half in range(2) for place in ORDER])
    theta = 2.0 * np.pi * (np.outer(bins, np.arange(PULSES)) % PULSES) / PULSES
    cosines, sines = np.cos(theta), np.sin(theta)
    real = np.concatenate([cosines, sines], axis=1)
    imag = np.concatenate([-sines, cosines], axis=1)
    return np.concatenate([real, imag], axis=0).astype(np.float32)


def range_band():
    source = np.arange(3 * LANES)[:, None] - LANES
    lane = np.arange(LANES)[None, :]
    lead, lag = lane - source, source - lane
    bands = [((d > 1) & (d <= REACH_R)) for d in (lead, lag)]
    return np.concatenate(bands, axis=1).astype(np.float32)


def doppler_bands(group):
    tables = []
    for offsets in ((3, 4), (2,)):
        table = np.zeros((2, group, BINS, group * (BINS + EDGE)), np.float32)
        for side, sign in enumerate((-1, 1)):
            for row in range(group):
                for slot, place in enumerate(ORDER):
                    for offset in offsets:
                        source = (place + sign * offset) % PULSES
                        spot = ORDER.index(source % BINS)
                        if source < BINS:
                            column = row * BINS + spot
                        else:
                            column = group * BINS + row * EDGE + spot
                        table[side, row, slot, column] += 1.0
        tables.append(table.reshape(2 * group * BINS, -1))
    return tables


GROUP = 8


def kernel(
    echoes,
    *refs,
):
    sources, (result, *scratch) = refs[:8], refs[8:]
    tables, (stage_sem, *scratch) = scratch[:8], scratch[8:]
    stages = []
    for index, (source, table) in enumerate(zip(sources, tables)):
        stage = pltpu.make_async_copy(source, table, stage_sem.at[index])
        stages.append(stage)
    body(echoes, result, stages, *tables, *scratch)


def body(
    echoes,
    result,
    stages,
    taper,
    trig,
    band,
    dop_far,
    dop_near,
    beam,
    blank,
    cfar,
    held,
    power,
    off,
    off_edge,
    on,
    on_edge,
    logs,
    logs_edge,
    center,
    weighted,
    level,
    inverse,
    load_sem,
    send_sem,
    recv_sem,
):
    az, rd = lax.axis_index("az"), lax.axis_index("rd")
    count = lax.axis_size("az")
    odd = lax.rem(az, 2)
    pair = (az, 1 - rd)
    outer = (lax.rem(az - 1 + 2 * odd + count, count), 1 - rd)
    inner = (az + 1 - 2 * odd, rd)

    def physical(row):
        return row + odd * (ROWS - 1 - 2 * row)

    def block_at(half, place):
        return OWN - 1 - place + half * (1 + 2 * place)

    loads = []
    for c in range(CHUNKS):
        first = (rd * c + (1 - rd) * (CHUNKS - 1 - c)) * WIDE
        load = pltpu.make_async_copy(
            echoes.at[:, :, :, pl.ds(pl.multiple_of(first, WIDE), WIDE)],
            held.at[c],
            load_sem.at[c],
        )
        loads.append(load)
    for stage in stages[:2]:
        stage.start()
    for load in loads:
        load.start()
    for stage in stages[2:]:
        stage.start()

    barrier = pltpu.get_barrier_semaphore()
    for target in (pair, outer, inner):
        pl.semaphore_signal(
            barrier, inc=1, device_id=target, device_id_type=pl.DeviceIdType.MESH
        )

    def transfer(c, kind, half):
        place, size = PIECES[c]
        blocks = pl.ds(half * OWN + place, size)
        what = kind if kind < PAIR_KINDS + 4 else kind - 4
        if what < PAIR_KINDS:
            bins, cut = (
                (0, (pl.ds(0, HALO),)),
                (0, (pl.ds(HALO, 2), pl.ds(0, EDGE))),
                (1, (pl.ds(0, 2), pl.ds(0, EDGE))),
                (1, (pl.ds(2, HALO),)),
                (1, (pl.ds(0, 2), pl.ds(EDGE, EDGE))),
            )[what]
            src = power.at[(bins, blocks) + cut]
            dst, target = power.at[(1 - bins, blocks) + cut], pair
        elif what == 5:
            src, dst, target = power.at[1, blocks, pl.ds(0, HALO)], off.at[blocks], outer
        elif what == 6:
            src = power.at[0, blocks, pl.ds(0, 2), pl.ds(0, EDGE)]
            dst, target = off_edge.at[blocks], outer
        elif what == 7:
            src = power.at[0, blocks, pl.ds(ROWS - HALO, HALO)]
            dst, target = on.at[blocks], inner
        else:
            src = power.at[1, blocks, pl.ds(ROWS - 2, 2), pl.ds(0, EDGE)]
            dst, target = on_edge.at[blocks], inner
        return pltpu.make_async_remote_copy(
            src_ref=src,
            dst_ref=dst,
            send_sem=send_sem.at[c, kind],
            recv_sem=recv_sem.at[c, kind],
            device_id=target,
            device_id_type=pl.DeviceIdType.MESH,
        )

    urgent = az == count - 1

    def send(c, *kinds):
        for kind in kinds:
            transfer(c, kind, rd if kind < PAIR_KINDS + 4 else 1 - rd).start()

    def receive(c, *kinds):
        for kind in kinds:
            other = kind < PAIR_KINDS + 2 or kind > PAIR_KINDS + 5
            transfer(c, kind, 1 - rd if other else rd).wait_recv()

    for stage in stages[:2]:
        stage.wait()
    lane_parity = lax.rem(lax.broadcasted_iota(jnp.int32, (1, PULSES), 1), 2)
    signs = 1.0 - (2 * rd * lane_parity).astype(F32)
    tapered = taper[...] * signs
    bank = (trig[...] * jnp.concatenate([tapered, tapered], axis=1)).astype(BF16)

    for c in range(CHUNKS):
        loads[c].wait()
        for row in range(ROWS):
            spot = physical(row)
            pulses = jnp.concatenate([held[c, 0, spot], held[c, 1, spot]], axis=0)
            spectrum = jnp.dot(bank, pulses, preferred_element_type=F32)
            real, imag = spectrum[:PULSES], spectrum[PULSES:]
            powers = (real * real + imag * imag).astype(BF16)
            for part in range(PER):
                place = c * PER + part * rd + (PER - 1 - part) * (1 - rd)
                for half in range(2):
                    power[half, rd * OWN + place, row] = powers[
                        half * BINS : (half + 1) * BINS, part * LANES : (part + 1) * LANES
                    ]
        if c == 0:
            pl.semaphore_wait(barrier, 3)
        for piece, (place, _) in enumerate(PIECES):
            if place // PER == c:
                send(piece, 0, 1, 2, 7, 8)

                if piece < AHEAD:
                    send(piece, 5, 6)
                else:

                    @pl.when(urgent)
                    def _():
                        send(piece, 5, 6)

                if piece > 0:

                    @pl.when(jnp.logical_not(urgent))
                    def _():
                        send(piece - 1, 3, 4)

    @pl.when(jnp.logical_not(urgent))
    def _():
        send(len(PIECES) - 1, 3, 4)

    @pl.when(urgent)
    def _():
        for piece in range(len(PIECES)):
            send(piece, 3, 4)


    for stage in stages[2:]:
        stage.wait()
    beams = [
        (beam[j] + odd.astype(F32) * (beam[4 - j] - beam[j])) * (1.0 / PULSES)
        for j in range(5)
    ]
    near_d = (2 - cfar[2]).astype(F32)
    near_a = (2 - cfar[4]).astype(F32)
    ones = jnp.ones((8, LANES), F32)
    scale_d = 1.0 / (ones * cfar[3].astype(F32))
    scale_d = jnp.concatenate([scale_d, scale_d], axis=0)
    scale_a = 1.0 / (ones * cfar[5].astype(F32))
    scale_a = jnp.concatenate([scale_a, scale_a], axis=0)
    doppler = (dop_far[...].astype(F32) + near_d * dop_near[...].astype(F32)).astype(BF16)

    lanes = lax.broadcasted_iota(jnp.int32, (8, LANES), 1)
    window = REACH_R - 1
    lead_in = jnp.clip(lanes - 1, 0, window).astype(F32)
    lag_in = jnp.clip(LANES - 2 - lanes, 0, window).astype(F32)
    lead_out, lag_out = window - lead_in, window - lag_in

    def weight_of(row, b):
        return blank[physical(row), b].astype(F32)

    @pl.loop(0, ROWS)
    def _(row):
        weights = [weight_of(row, b) for b in range(BLOCKS)]
        for b in range(BLOCKS):
            lead, lag = weights[b] * lead_in, weights[b] * lag_in
            if b > 0:
                lead = lead + weights[b - 1] * lead_out
            if b < BLOCKS - 1:
                lag = lag + weights[b + 1] * lag_out
            inverse[0, b, row] = 1.0 / jnp.maximum(lead, 1.0)
            inverse[1, b, row] = 1.0 / jnp.maximum(lag, 1.0)

    for edge in (0, BLOCKS + 1):
        weighted[edge] = jnp.zeros((ROWS, BINS, LANES), BF16)

    def integrate(rows, put):
        held_rows = [rows(e) for e in range(4)]
        last = None
        for t in range(put.count):
            held_rows.append(rows(t + 4))
            total = beams[0] * held_rows[0]
            for j in range(1, 5):
                total = total + beams[j] * held_rows[j]
            put(t, jnp.log(total + 0.05))
            held_rows.pop(0)

    def level_block(half, place):
        b, q = block_at(half, place), half * OWN + place

        def rows(e):
            if e < HALO:
                return off[q, HALO - 1 - e].astype(F32)
            if e < HALO + ROWS:
                return power[0, q, e - HALO].astype(F32)
            return on[q, 2 * HALO + ROWS - 1 - e].astype(F32)

        def put(t, value):
            logs[t] = value
            row = t - REACH_A
            if 0 <= row < ROWS:
                rounded = value.astype(BF16)
                center[b, row] = rounded
                weighted[b + 1, row] = (
                    rounded.astype(F32) * weight_of(row, b)
                ).astype(BF16)

        put.count = SPAN
        integrate(rows, put)

        def edge_rows(e):
            if e < 2:
                return off_edge[q, 1 - e].astype(F32)
            if e < 2 + ROWS:
                return power[1, q, e - 2, 0:EDGE].astype(F32)
            return on_edge[q, 1 - (e - 2 - ROWS)].astype(F32)

        waiting = []

        def put_edge(t, value):
            waiting.append(value)
            if t % 2 == 1:
                logs_edge[t // 2] = jnp.concatenate(waiting, axis=0).astype(BF16)
                waiting.clear()

        put_edge.count = ROWS
        integrate(edge_rows, put_edge)

        means = []
        for group in range(ROWS // GROUP):
            stacked = jnp.concatenate(
                [
                    center[b, group * GROUP : (group + 1) * GROUP].reshape(
                        GROUP * BINS, LANES
                    ),
                    logs_edge[group * GROUP // 2 : (group + 1) * GROUP // 2].reshape(
                        GROUP * EDGE, LANES
                    ),
                ],
                axis=0,
            )
            sums = jnp.dot(doppler, stacked, preferred_element_type=F32)
            size = GROUP * BINS
            means.append(jnp.maximum(sums[:size], sums[size:]))

        far = REACH_A - 2
        lead = logs[0]
        lag = logs[REACH_A + 3]
        for d in range(1, far):
            lead = lead + logs[d]
            lag = lag + logs[REACH_A + 3 + d]
        for row in range(ROWS):
            azimuth = jnp.maximum(
                lead + near_a * logs[row + far], lag + near_a * logs[row + REACH_A + 2]
            )
            local = row % GROUP
            mean = means[row // GROUP][local * BINS : (local + 1) * BINS]
            level[b, row] = jnp.maximum(azimuth * scale_a, mean * scale_d)
            if row < ROWS - 1:
                lead = lead + (logs[row + far] - logs[row])
                lag = lag + (logs[row + REACH_A + 3 + far] - logs[row + REACH_A + 3])

    low = lax.broadcasted_iota(jnp.int32, (8, LANES), 0) < 4

    def finish_block(b):
        cells = pl.ds(pl.multiple_of(b * LANES, LANES), LANES)
        stacked = jnp.concatenate(
            [weighted[b + i].reshape(ROWS * BINS, LANES) for i in range(3)], axis=1
        )
        sums = jnp.dot(stacked, band[...], preferred_element_type=F32)
        for row in range(ROWS):
            here = slice(row * BINS, (row + 1) * BINS)
            lead, lag = inverse[0, b, row], inverse[1, b, row]
            lead = sums[here, :LANES] * jnp.concatenate([lead, lead], axis=0)
            lag = sums[here, LANES:] * jnp.concatenate([lag, lag], axis=0)
            noise = jnp.maximum(jnp.maximum(lead, lag), level[b, row])
            excess = weight_of(row, b) * (center[b, row].astype(F32) - noise)
            first, second = excess[:8], pltpu.roll(excess[8:], 4, 0)
            ordered = jnp.concatenate(
                [jnp.where(low, first, second), jnp.where(low, second, first)], axis=0
            )
            result[physical(row), :, cells] = ordered.astype(BF16)

    def levels(c, half):
        place, size = PIECES[c]

        @pl.loop(0, size)
        def _(index):
            level_block(half, place + index)

    def finishes(c, half):
        place, size = PIECES[c]
        last = place + size - (c < len(PIECES) - 1)
        for each in range(max(place - 1, 0), last):
            finish_block(block_at(half, each))

    def relay(c):
        if c < len(PIECES):
            receive(c, 0, 1, 2)
            send(c, 9, 10)
        if c + AHEAD < len(PIECES):

            @pl.when(jnp.logical_not(urgent))
            def _():
                send(c + AHEAD, 5, 6)

    for c in range(AHEAD):
        relay(c)

    @pl.when(urgent)
    def _():
        for c in range(AHEAD, len(PIECES)):
            relay(c)

    for c in range(len(PIECES)):
        receive(c, 3, 4)
        send(c, 11, 12)
        receive(c, 9, 10, 7, 8)
        levels(c, rd)
        if c > 0:
            finishes(c, rd)

        @pl.when(jnp.logical_not(urgent))
        def _():
            relay(c + AHEAD)

        receive(c, 11, 12, 5, 6)
        levels(c, 1 - rd)
        if c == 0:
            finishes(c, rd)
        finishes(c, 1 - rd)

    for c in range(len(PIECES)):
        for kind in range(KINDS):
            transfer(c, kind, rd if kind < PAIR_KINDS + 4 else 1 - rd).wait_send()


def local(echoes, pulse_taper, beam_weights, blanking, cfar_sizes):
    far, near = doppler_bands(GROUP)
    hbm = pl.BlockSpec(memory_space=pltpu.HBM)
    return pl.pallas_call(
        kernel,
        out_shape=jax.ShapeDtypeStruct((ROWS, BINS, BLOCKS * LANES), BF16),
        in_specs=[hbm] * 9,
        out_specs=pl.BlockSpec(memory_space=pltpu.VMEM),
        scratch_shapes=[
            pltpu.VMEM((1, PULSES), F32),
            pltpu.VMEM((2 * PULSES, 2 * PULSES), F32),
            pltpu.VMEM((3 * LANES, 2 * LANES), BF16),
            pltpu.VMEM((2 * GROUP * BINS, GROUP * (BINS + EDGE)), BF16),
            pltpu.VMEM((2 * GROUP * BINS, GROUP * (BINS + EDGE)), BF16),
            pltpu.SMEM((5,), F32),
            pltpu.SMEM((ROWS, BLOCKS), jnp.int32),
            pltpu.SMEM((6,), jnp.int32),
            pltpu.SemaphoreType.DMA((8,)),
            pltpu.VMEM((CHUNKS, 2, ROWS, PULSES, WIDE), BF16),
            pltpu.VMEM((2, BLOCKS, ROWS, BINS, LANES), BF16),
            pltpu.VMEM((BLOCKS, HALO, BINS, LANES), BF16),
            pltpu.VMEM((BLOCKS, 2, EDGE, LANES), BF16),
            pltpu.VMEM((BLOCKS, HALO, BINS, LANES), BF16),
            pltpu.VMEM((BLOCKS, 2, EDGE, LANES), BF16),
            pltpu.VMEM((SPAN, BINS, LANES), F32),
            pltpu.VMEM((ROWS // 2, BINS, LANES), BF16),
            pltpu.VMEM((BLOCKS, ROWS, BINS, LANES), BF16),
            pltpu.VMEM((BLOCKS + 2, ROWS, BINS, LANES), BF16),
            pltpu.VMEM((BLOCKS, ROWS, BINS, LANES), F32),
            pltpu.VMEM((2, BLOCKS, ROWS, 8, LANES), F32),
            pltpu.SemaphoreType.DMA((CHUNKS,)),
            pltpu.SemaphoreType.DMA((len(PIECES), KINDS)),
            pltpu.SemaphoreType.DMA((len(PIECES), KINDS)),
        ],
        compiler_params=pltpu.CompilerParams(
            collective_id=0, has_side_effects=True, vmem_limit_bytes=48<<20
        ),
    )(
        *(pltpu.with_memory_space_constraint(x, pltpu.HBM) for x in (
        echoes,
        pulse_taper.reshape(1, PULSES),
        jnp.asarray(trig_table()),
        jnp.asarray(range_band(), BF16),
        jnp.asarray(far, BF16),
        jnp.asarray(near, BF16),
        beam_weights,
        blanking,
        cfar_sizes,
        ))
    )


def solution(mesh):
    in_specs = (P(None, "az", None, "rd"), P(), P(), P("az", None), P())
    out_specs = P("az", "rd", None)
    return jax.shard_map(local, mesh=mesh, in_specs=in_specs, out_specs=out_specs, check_vma=False)
```

```python
import math

import jax
import jax.numpy as jnp
import numpy as np
from jax import lax
from jax.experimental import pallas as pl
from jax.experimental.pallas import tpu as pltpu
from jax.sharding import PartitionSpec as P

F32 = jnp.float32
BF16 = jnp.bfloat16
PULSES = 32
ROWS = 16
BINS = 16
LANES = 128
BLOCKS = 16
OWN = 8
CHUNKS = 4
PER = OWN // CHUNKS
WIDE = PER * LANES
REACH_R = 24
REACH_D = 4
REACH_A = 12
HALO = REACH_A + 2
SPAN = ROWS + 2 * REACH_A
ORDER = (0, 1, 2, 3, 12, 13, 14, 15, 4, 5, 6, 7, 8, 9, 10, 11)
EDGE = 8
PIECES = ((0, 2), (2, 2), (4, 2), (6, 1), (7, 1))
AHEAD = 2
PAIR_KINDS, KINDS = 5, 13


def trig_table():
    bins = np.array([half * BINS + place for half in range(2) for place in ORDER])
    theta = 2.0 * np.pi * (np.outer(bins, np.arange(PULSES)) % PULSES) / PULSES
    cosines, sines = np.cos(theta), np.sin(theta)
    real = np.concatenate([cosines, sines], axis=1)
    imag = np.concatenate([-sines, cosines], axis=1)
    return np.concatenate([real, imag], axis=0).astype(np.float32)


def range_band():
    source = np.arange(3 * LANES)[:, None] - LANES
    lane = np.arange(LANES)[None, :]
    lead, lag = lane - source, source - lane
    bands = [((d > 1) & (d <= REACH_R)) for d in (lead, lag)]
    return np.concatenate(bands, axis=1).astype(np.float32)


def doppler_bands(group):
    tables = []
    for offsets in ((3, 4), (2,)):
        table = np.zeros((2, group, BINS, group * (BINS + EDGE)), np.float32)
        for side, sign in enumerate((-1, 1)):
            for row in range(group):
                for slot, place in enumerate(ORDER):
                    for offset in offsets:
                        source = (place + sign * offset) % PULSES
                        spot = ORDER.index(source % BINS)
                        if source < BINS:
                            column = row * BINS + spot
                        else:
                            column = group * BINS + row * EDGE + spot
                        table[side, row, slot, column] += 1.0
        tables.append(table.reshape(2 * group * BINS, -1))
    return tables


GROUP = 8


def kernel(
    echoes,
    *refs,
):
    sources, (result, *scratch) = refs[:8], refs[8:]
    tables, (stage_sem, *scratch) = scratch[:8], scratch[8:]
    stages = []
    for index, (source, table) in enumerate(zip(sources, tables)):
        stage = pltpu.make_async_copy(source, table, stage_sem.at[index])
        stages.append(stage)
    body(echoes, result, stages, *tables, *scratch)


def body(
    echoes,
    result,
    stages,
    taper,
    trig,
    band,
    dop_far,
    dop_near,
    beam,
    blank,
    cfar,
    held,
    power,
    off,
    off_edge,
    on,
    on_edge,
    logs,
    logs_edge,
    center,
    weighted,
    level,
    inverse,
    load_sem,
    send_sem,
    recv_sem,
):
    az, rd = lax.axis_index("az"), lax.axis_index("rd")
    count = lax.axis_size("az")
    odd = lax.rem(az, 2)
    pair = (az, 1 - rd)
    outer = (lax.rem(az - 1 + 2 * odd + count, count), 1 - rd)
    inner = (az + 1 - 2 * odd, rd)

    def physical(row):
        return row + odd * (ROWS - 1 - 2 * row)

    def block_at(half, place):
        return OWN - 1 - place + half * (1 + 2 * place)

    loads = []
    for c in range(CHUNKS):
        first = (rd * c + (1 - rd) * (CHUNKS - 1 - c)) * WIDE
        load = pltpu.make_async_copy(
            echoes.at[:, :, :, pl.ds(pl.multiple_of(first, WIDE), WIDE)],
            held.at[c],
            load_sem.at[c],
        )
        loads.append(load)
    for stage in stages[:2]:
        stage.start()
    for load in loads:
        load.start()
    for stage in stages[2:]:
        stage.start()

    barrier = pltpu.get_barrier_semaphore()
    for target in (pair, outer, inner):
        pl.semaphore_signal(
            barrier, inc=1, device_id=target, device_id_type=pl.DeviceIdType.MESH
        )

    def transfer(c, kind, half):
        place, size = PIECES[c]
        blocks = pl.ds(half * OWN + place, size)
        what = kind if kind < PAIR_KINDS + 4 else kind - 4
        if what < PAIR_KINDS:
            bins, cut = (
                (0, (pl.ds(0, HALO),)),
                (0, (pl.ds(HALO, 2), pl.ds(0, EDGE))),
                (1, (pl.ds(0, 2), pl.ds(0, EDGE))),
                (1, (pl.ds(2, HALO),)),
                (1, (pl.ds(0, 2), pl.ds(EDGE, EDGE))),
            )[what]
            src = power.at[(bins, blocks) + cut]
            dst, target = power.at[(1 - bins, blocks) + cut], pair
        elif what == 5:
            src, dst, target = power.at[1, blocks, pl.ds(0, HALO)], off.at[blocks], outer
        elif what == 6:
            src = power.at[0, blocks, pl.ds(0, 2), pl.ds(0, EDGE)]
            dst, target = off_edge.at[blocks], outer
        elif what == 7:
            src = power.at[0, blocks, pl.ds(ROWS - HALO, HALO)]
            dst, target = on.at[blocks], inner
        else:
            src = power.at[1, blocks, pl.ds(ROWS - 2, 2), pl.ds(0, EDGE)]
            dst, target = on_edge.at[blocks], inner
        return pltpu.make_async_remote_copy(
            src_ref=src,
            dst_ref=dst,
            send_sem=send_sem.at[c, kind],
            recv_sem=recv_sem.at[c, kind],
            device_id=target,
            device_id_type=pl.DeviceIdType.MESH,
        )

    urgent = az == count - 1

    def send(c, *kinds):
        for kind in kinds:
            transfer(c, kind, rd if kind < PAIR_KINDS + 4 else 1 - rd).start()

    def receive(c, *kinds):
        for kind in kinds:
            other = kind < PAIR_KINDS + 2 or kind > PAIR_KINDS + 5
            transfer(c, kind, 1 - rd if other else rd).wait_recv()

    for stage in stages[:2]:
        stage.wait()
    lane_parity = lax.rem(lax.broadcasted_iota(jnp.int32, (1, PULSES), 1), 2)
    signs = 1.0 - (2 * rd * lane_parity).astype(F32)
    tapered = taper[...] * signs
    bank = (trig[...] * jnp.concatenate([tapered, tapered], axis=1)).astype(BF16)

    for c in range(CHUNKS):
        loads[c].wait()
        for row in range(ROWS):
            spot = physical(row)
            pulses = jnp.concatenate([held[c, 0, spot], held[c, 1, spot]], axis=0)
            spectrum = jnp.dot(bank, pulses, preferred_element_type=F32)
            real, imag = spectrum[:PULSES], spectrum[PULSES:]
            powers = (real * real + imag * imag).astype(BF16)
            for part in range(PER):
                place = c * PER + part * rd + (PER - 1 - part) * (1 - rd)
                for half in range(2):
                    power[half, rd * OWN + place, row] = powers[
                        half * BINS : (half + 1) * BINS, part * LANES : (part + 1) * LANES
                    ]
        if c == 0:
            pl.semaphore_wait(barrier, 3)
        for piece, (place, _) in enumerate(PIECES):
            if place // PER == c:
                send(piece, 0, 1, 2, 7, 8)

                if piece < AHEAD:
                    send(piece, 5, 6)
                else:

                    @pl.when(urgent)
                    def _():
                        send(piece, 5, 6)

                if piece > 0:

                    @pl.when(jnp.logical_not(urgent))
                    def _():
                        send(piece - 1, 3, 4)

    @pl.when(jnp.logical_not(urgent))
    def _():
        send(len(PIECES) - 1, 3, 4)

    @pl.when(urgent)
    def _():
        for piece in range(len(PIECES)):
            send(piece, 3, 4)


    for stage in stages[2:]:
        stage.wait()
    beams = [
        (beam[j] + odd.astype(F32) * (beam[4 - j] - beam[j])) * (1.0 / PULSES)
        for j in range(5)
    ]
    near_d = (2 - cfar[2]).astype(F32)
    near_a = (2 - cfar[4]).astype(F32)
    ones = jnp.ones((8, LANES), F32)
    scale_d = 1.0 / (ones * cfar[3].astype(F32))
    scale_d = jnp.concatenate([scale_d, scale_d], axis=0)
    scale_a = 1.0 / (ones * cfar[5].astype(F32))
    scale_a = jnp.concatenate([scale_a, scale_a], axis=0)
    doppler = (dop_far[...].astype(F32) + near_d * dop_near[...].astype(F32)).astype(BF16)

    lanes = lax.broadcasted_iota(jnp.int32, (8, LANES), 1)
    window = REACH_R - 1
    lead_in = jnp.clip(lanes - 1, 0, window).astype(F32)
    lag_in = jnp.clip(LANES - 2 - lanes, 0, window).astype(F32)
    lead_out, lag_out = window - lead_in, window - lag_in

    def weight_of(row, b):
        return blank[physical(row), b].astype(F32)

    @pl.loop(0, ROWS)
    def _(row):
        weights = [weight_of(row, b) for b in range(BLOCKS)]
        for b in range(BLOCKS):
            lead, lag = weights[b] * lead_in, weights[b] * lag_in
            if b > 0:
                lead = lead + weights[b - 1] * lead_out
            if b < BLOCKS - 1:
                lag = lag + weights[b + 1] * lag_out
            inverse[0, b, row] = 1.0 / jnp.maximum(lead, 1.0)
            inverse[1, b, row] = 1.0 / jnp.maximum(lag, 1.0)

    for edge in (0, BLOCKS + 1):
        weighted[edge] = jnp.zeros((ROWS, BINS, LANES), BF16)

    def integrate(rows, put, first, end):
        held_rows = [rows(first + e) for e in range(4)]
        for t in range(first, end):
            held_rows.append(rows(t + 4))
            total = beams[0] * held_rows[0]
            for j in range(1, 5):
                total = total + beams[j] * held_rows[j]
            put(t, jnp.log(total + 0.05))
            held_rows.pop(0)

    def logs_of(half, place, firsts, ends):
        b, q = block_at(half, place), half * OWN + place

        def rows(e):
            if e < HALO:
                return off[q, HALO - 1 - e].astype(F32)
            if e < HALO + ROWS:
                return power[0, q, e - HALO].astype(F32)
            return on[q, 2 * HALO + ROWS - 1 - e].astype(F32)

        def put(t, value):
            logs[q, t] = value
            row = t - REACH_A
            if 0 <= row < ROWS:
                rounded = value.astype(BF16)
                center[b, row] = rounded
                weighted[b + 1, row] = (
                    rounded.astype(F32) * weight_of(row, b)
                ).astype(BF16)

        integrate(rows, put, firsts[0], ends[0])

        def edge_rows(e):
            if e < 2:
                return off_edge[q, 1 - e].astype(F32)
            if e < 2 + ROWS:
                return power[1, q, e - 2, 0:EDGE].astype(F32)
            return on_edge[q, 1 - (e - 2 - ROWS)].astype(F32)

        waiting = []

        def put_edge(t, value):
            waiting.append(value)
            if t % 2 == 1:
                logs_edge[q, t // 2] = jnp.concatenate(waiting, axis=0).astype(BF16)
                waiting.clear()

        integrate(edge_rows, put_edge, firsts[1], ends[1])

    def level_block(half, place):
        b, q = block_at(half, place), half * OWN + place

        means = []
        for group in range(ROWS // GROUP):
            stacked = jnp.concatenate(
                [
                    center[b, group * GROUP : (group + 1) * GROUP].reshape(
                        GROUP * BINS, LANES
                    ),
                    logs_edge[q, group * GROUP // 2 : (group + 1) * GROUP // 2].reshape(
                        GROUP * EDGE, LANES
                    ),
                ],
                axis=0,
            )
            sums = jnp.dot(doppler, stacked, preferred_element_type=F32)
            size = GROUP * BINS
            means.append(jnp.maximum(sums[:size], sums[size:]))

        far = REACH_A - 2
        lead = logs[q, 0]
        lag = logs[q, REACH_A + 3]
        for d in range(1, far):
            lead = lead + logs[q, d]
            lag = lag + logs[q, REACH_A + 3 + d]
        for row in range(ROWS):
            azimuth = jnp.maximum(
                lead + near_a * logs[q, row + far], lag + near_a * logs[q, row + REACH_A + 2]
            )
            local = row % GROUP
            mean = means[row // GROUP][local * BINS : (local + 1) * BINS]
            level[b, row] = jnp.maximum(azimuth * scale_a, mean * scale_d)
            if row < ROWS - 1:
                lead = lead + (logs[q, row + far] - logs[q, row])
                lag = lag + (logs[q, row + REACH_A + 3 + far] - logs[q, row + REACH_A + 3])

    low = lax.broadcasted_iota(jnp.int32, (8, LANES), 0) < 4

    def finish_block(b):
        cells = pl.ds(pl.multiple_of(b * LANES, LANES), LANES)
        stacked = jnp.concatenate(
            [weighted[b + i].reshape(ROWS * BINS, LANES) for i in range(3)], axis=1
        )
        sums = jnp.dot(stacked, band[...], preferred_element_type=F32)
        for row in range(ROWS):
            here = slice(row * BINS, (row + 1) * BINS)
            lead, lag = inverse[0, b, row], inverse[1, b, row]
            lead = sums[here, :LANES] * jnp.concatenate([lead, lead], axis=0)
            lag = sums[here, LANES:] * jnp.concatenate([lag, lag], axis=0)
            noise = jnp.maximum(jnp.maximum(lead, lag), level[b, row])
            excess = weight_of(row, b) * (center[b, row].astype(F32) - noise)
            first, second = excess[:8], pltpu.roll(excess[8:], 4, 0)
            ordered = jnp.concatenate(
                [jnp.where(low, first, second), jnp.where(low, second, first)], axis=0
            )
            result[physical(row), :, cells] = ordered.astype(BF16)

    def levels(c, half, ends):
        place, size = PIECES[c]

        @pl.loop(0, size)
        def _(index):
            logs_of(half, place + index, (0, 0), ends)
            level_block(half, place + index)

    def finishes(c, half):
        place, size = PIECES[c]
        last = place + size - (c < len(PIECES) - 1)
        for each in range(max(place - 1, 0), last):
            finish_block(block_at(half, each))

    def relay(c):
        if c < len(PIECES):
            receive(c, 0, 1, 2)
            send(c, 9, 10)
        if c + AHEAD < len(PIECES):

            @pl.when(jnp.logical_not(urgent))
            def _():
                send(c + AHEAD, 5, 6)

    for c in range(AHEAD):
        relay(c)

    @pl.when(urgent)
    def _():
        for c in range(AHEAD, len(PIECES)):
            relay(c)

    for c in range(len(PIECES)):
        receive(c, 7, 8)

    @pl.loop(0, OWN)
    def _(place):
        logs_of(rd, place, (HALO, 2), (SPAN, ROWS))

    for c in range(len(PIECES)):
        receive(c, 3, 4)
        send(c, 11, 12)
        receive(c, 9, 10)
        levels(c, rd, (HALO, 2))
        if c > 0:
            finishes(c, rd)

        @pl.when(jnp.logical_not(urgent))
        def _():
            relay(c + AHEAD)

        receive(c, 11, 12, 5, 6)
        levels(c, 1 - rd, (SPAN, ROWS))
        if c == 0:
            finishes(c, rd)
        finishes(c, 1 - rd)

    for c in range(len(PIECES)):
        for kind in range(KINDS):
            transfer(c, kind, rd if kind < PAIR_KINDS + 4 else 1 - rd).wait_send()


def local(echoes, pulse_taper, beam_weights, blanking, cfar_sizes):
    far, near = doppler_bands(GROUP)
    hbm = pl.BlockSpec(memory_space=pltpu.HBM)
    return pl.pallas_call(
        kernel,
        out_shape=jax.ShapeDtypeStruct((ROWS, BINS, BLOCKS * LANES), BF16),
        in_specs=[hbm] * 9,
        out_specs=pl.BlockSpec(memory_space=pltpu.VMEM),
        scratch_shapes=[
            pltpu.VMEM((1, PULSES), F32),
            pltpu.VMEM((2 * PULSES, 2 * PULSES), F32),
            pltpu.VMEM((3 * LANES, 2 * LANES), BF16),
            pltpu.VMEM((2 * GROUP * BINS, GROUP * (BINS + EDGE)), BF16),
            pltpu.VMEM((2 * GROUP * BINS, GROUP * (BINS + EDGE)), BF16),
            pltpu.SMEM((5,), F32),
            pltpu.SMEM((ROWS, BLOCKS), jnp.int32),
            pltpu.SMEM((6,), jnp.int32),
            pltpu.SemaphoreType.DMA((8,)),
            pltpu.VMEM((CHUNKS, 2, ROWS, PULSES, WIDE), BF16),
            pltpu.VMEM((2, BLOCKS, ROWS, BINS, LANES), BF16),
            pltpu.VMEM((BLOCKS, HALO, BINS, LANES), BF16),
            pltpu.VMEM((BLOCKS, 2, EDGE, LANES), BF16),
            pltpu.VMEM((BLOCKS, HALO, BINS, LANES), BF16),
            pltpu.VMEM((BLOCKS, 2, EDGE, LANES), BF16),
            pltpu.VMEM((BLOCKS, SPAN, BINS, LANES), F32),
            pltpu.VMEM((BLOCKS, ROWS // 2, BINS, LANES), BF16),
            pltpu.VMEM((BLOCKS, ROWS, BINS, LANES), BF16),
            pltpu.VMEM((BLOCKS + 2, ROWS, BINS, LANES), BF16),
            pltpu.VMEM((BLOCKS, ROWS, BINS, LANES), F32),
            pltpu.VMEM((2, BLOCKS, ROWS, 8, LANES), F32),
            pltpu.SemaphoreType.DMA((CHUNKS,)),
            pltpu.SemaphoreType.DMA((len(PIECES), KINDS)),
            pltpu.SemaphoreType.DMA((len(PIECES), KINDS)),
        ],
        compiler_params=pltpu.CompilerParams(
            collective_id=0, has_side_effects=True, vmem_limit_bytes=48<<20
        ),
    )(
        *(pltpu.with_memory_space_constraint(x, pltpu.HBM) for x in (
        echoes,
        pulse_taper.reshape(1, PULSES),
        jnp.asarray(trig_table()),
        jnp.asarray(range_band(), BF16),
        jnp.asarray(far, BF16),
        jnp.asarray(near, BF16),
        beam_weights,
        blanking,
        cfar_sizes,
        ))
    )


def solution(mesh):
    in_specs = (P(None, "az", None, "rd"), P(), P(), P("az", None), P())
    out_specs = P("az", "rd", None)
    return jax.shard_map(local, mesh=mesh, in_specs=in_specs, out_specs=out_specs, check_vma=False)
```

```python
import math

import jax
import jax.numpy as jnp
import numpy as np
from jax import lax
from jax.experimental import pallas as pl
from jax.experimental.pallas import tpu as pltpu
from jax.sharding import PartitionSpec as P

F32 = jnp.float32
BF16 = jnp.bfloat16
PULSES = 32
ROWS = 16
BINS = 16
LANES = 128
BLOCKS = 16
OWN = 8
CHUNKS = 4
PER = OWN // CHUNKS
WIDE = PER * LANES
REACH_R = 24
REACH_D = 4
REACH_A = 12
HALO = REACH_A + 2
SPAN = ROWS + 2 * REACH_A
ORDER = (0, 1, 2, 3, 12, 13, 14, 15, 4, 5, 6, 7, 8, 9, 10, 11)
EDGE = 8
PIECES = ((0, 2), (2, 2), (4, 2), (6, 2))
AHEAD = 2
PAIR_KINDS, KINDS = 5, 13


def trig_table():
    bins = np.array([half * BINS + place for half in range(2) for place in ORDER])
    theta = 2.0 * np.pi * (np.outer(bins, np.arange(PULSES)) % PULSES) / PULSES
    cosines, sines = np.cos(theta), np.sin(theta)
    real = np.concatenate([cosines, sines], axis=1)
    imag = np.concatenate([-sines, cosines], axis=1)
    return np.concatenate([real, imag], axis=0).astype(np.float32)


def range_band():
    source = np.arange(3 * LANES)[:, None] - LANES
    lane = np.arange(LANES)[None, :]
    lead, lag = lane - source, source - lane
    bands = [((d > 1) & (d <= REACH_R)) for d in (lead, lag)]
    return np.concatenate(bands, axis=1).astype(np.float32)


def doppler_bands(group):
    tables = []
    for offsets in ((3, 4), (2,)):
        table = np.zeros((2, group, BINS, group * (BINS + EDGE)), np.float32)
        for side, sign in enumerate((-1, 1)):
            for row in range(group):
                for slot, place in enumerate(ORDER):
                    for offset in offsets:
                        source = (place + sign * offset) % PULSES
                        spot = ORDER.index(source % BINS)
                        if source < BINS:
                            column = row * BINS + spot
                        else:
                            column = group * BINS + row * EDGE + spot
                        table[side, row, slot, column] += 1.0
        tables.append(table.reshape(2 * group * BINS, -1))
    return tables


GROUP = 8


def kernel(
    echoes,
    *refs,
):
    sources, (result, *scratch) = refs[:8], refs[8:]
    tables, (stage_sem, *scratch) = scratch[:8], scratch[8:]
    stages = []
    for index, (source, table) in enumerate(zip(sources, tables)):
        stage = pltpu.make_async_copy(source, table, stage_sem.at[index])
        stages.append(stage)
    body(echoes, result, stages, *tables, *scratch)


def body(
    echoes,
    result,
    stages,
    taper,
    trig,
    band,
    dop_far,
    dop_near,
    beam,
    blank,
    cfar,
    held,
    power,
    off,
    off_edge,
    on,
    on_edge,
    logs,
    logs_edge,
    center,
    weighted,
    level,
    inverse,
    load_sem,
    send_sem,
    recv_sem,
):
    az, rd = lax.axis_index("az"), lax.axis_index("rd")
    count = lax.axis_size("az")
    odd = lax.rem(az, 2)
    pair = (az, 1 - rd)
    outer = (lax.rem(az - 1 + 2 * odd + count, count), 1 - rd)
    inner = (az + 1 - 2 * odd, rd)

    def physical(row):
        return row + odd * (ROWS - 1 - 2 * row)

    def block_at(half, place):
        return OWN - 1 - place + half * (1 + 2 * place)

    loads = []
    for c in range(CHUNKS):
        first = (rd * c + (1 - rd) * (CHUNKS - 1 - c)) * WIDE
        load = pltpu.make_async_copy(
            echoes.at[:, :, :, pl.ds(pl.multiple_of(first, WIDE), WIDE)],
            held.at[c],
            load_sem.at[c],
        )
        loads.append(load)
    for stage in stages[:2]:
        stage.start()
    for load in loads:
        load.start()
    for stage in stages[2:]:
        stage.start()

    barrier = pltpu.get_barrier_semaphore()
    for target in (pair, outer, inner):
        pl.semaphore_signal(
            barrier, inc=1, device_id=target, device_id_type=pl.DeviceIdType.MESH
        )

    def transfer(c, kind, half):
        place, size = PIECES[c]
        blocks = pl.ds(half * OWN + place, size)
        what = kind if kind < PAIR_KINDS + 4 else kind - 4
        if what < PAIR_KINDS:
            bins, cut = (
                (0, (pl.ds(0, HALO),)),
                (0, (pl.ds(HALO, 2), pl.ds(0, EDGE))),
                (1, (pl.ds(0, 2), pl.ds(0, EDGE))),
                (1, (pl.ds(2, HALO),)),
                (1, (pl.ds(0, 2), pl.ds(EDGE, EDGE))),
            )[what]
            src = power.at[(bins, blocks) + cut]
            dst, target = power.at[(1 - bins, blocks) + cut], pair
        elif what == 5:
            src, dst, target = power.at[1, blocks, pl.ds(0, HALO)], off.at[blocks], outer
        elif what == 6:
            src = power.at[0, blocks, pl.ds(0, 2), pl.ds(0, EDGE)]
            dst, target = off_edge.at[blocks], outer
        elif what == 7:
            src = power.at[0, blocks, pl.ds(ROWS - HALO, HALO)]
            dst, target = on.at[blocks], inner
        else:
            src = power.at[1, blocks, pl.ds(ROWS - 2, 2), pl.ds(0, EDGE)]
            dst, target = on_edge.at[blocks], inner
        return pltpu.make_async_remote_copy(
            src_ref=src,
            dst_ref=dst,
            send_sem=send_sem.at[c, kind],
            recv_sem=recv_sem.at[c, kind],
            device_id=target,
            device_id_type=pl.DeviceIdType.MESH,
        )

    urgent = az == count - 1

    def send(c, *kinds):
        for kind in kinds:
            transfer(c, kind, rd if kind < PAIR_KINDS + 4 else 1 - rd).start()

    def receive(c, *kinds):
        for kind in kinds:
            other = kind < PAIR_KINDS + 2 or kind > PAIR_KINDS + 5
            transfer(c, kind, 1 - rd if other else rd).wait_recv()

    for stage in stages[:2]:
        stage.wait()
    lane_parity = lax.rem(lax.broadcasted_iota(jnp.int32, (1, PULSES), 1), 2)
    signs = 1.0 - (2 * rd * lane_parity).astype(F32)
    tapered = taper[...] * signs
    bank = (trig[...] * jnp.concatenate([tapered, tapered], axis=1)).astype(BF16)

    for c in range(CHUNKS):
        loads[c].wait()
        for row in range(ROWS):
            spot = physical(row)
            pulses = jnp.concatenate([held[c, 0, spot], held[c, 1, spot]], axis=0)
            spectrum = jnp.dot(bank, pulses, preferred_element_type=F32)
            real, imag = spectrum[:PULSES], spectrum[PULSES:]
            powers = (real * real + imag * imag).astype(BF16)
            for part in range(PER):
                place = c * PER + part * rd + (PER - 1 - part) * (1 - rd)
                for half in range(2):
                    power[half, rd * OWN + place, row] = powers[
                        half * BINS : (half + 1) * BINS, part * LANES : (part + 1) * LANES
                    ]
        if c == 0:
            pl.semaphore_wait(barrier, 3)
        for piece, (place, _) in enumerate(PIECES):
            if place // PER == c:
                send(piece, 0, 1, 2, 7, 8)

                if piece < AHEAD:
                    send(piece, 5, 6)
                else:

                    @pl.when(urgent)
                    def _():
                        send(piece, 5, 6)

                if piece > 0:

                    @pl.when(jnp.logical_not(urgent))
                    def _():
                        send(piece - 1, 3, 4)

    @pl.when(jnp.logical_not(urgent))
    def _():
        send(len(PIECES) - 1, 3, 4)

    @pl.when(urgent)
    def _():
        for piece in range(len(PIECES)):
            send(piece, 3, 4)


    for stage in stages[2:]:
        stage.wait()
    beams = [
        (beam[j] + odd.astype(F32) * (beam[4 - j] - beam[j])) * (1.0 / PULSES)
        for j in range(5)
    ]
    near_d = (2 - cfar[2]).astype(F32)
    near_a = (2 - cfar[4]).astype(F32)
    ones = jnp.ones((8, LANES), F32)
    scale_d = 1.0 / (ones * cfar[3].astype(F32))
    scale_d = jnp.concatenate([scale_d, scale_d], axis=0)
    scale_a = 1.0 / (ones * cfar[5].astype(F32))
    scale_a = jnp.concatenate([scale_a, scale_a], axis=0)
    doppler = (dop_far[...].astype(F32) + near_d * dop_near[...].astype(F32)).astype(BF16)

    lanes = lax.broadcasted_iota(jnp.int32, (8, LANES), 1)
    window = REACH_R - 1
    lead_in = jnp.clip(lanes - 1, 0, window).astype(F32)
    lag_in = jnp.clip(LANES - 2 - lanes, 0, window).astype(F32)
    lead_out, lag_out = window - lead_in, window - lag_in

    def weight_of(row, b):
        return blank[physical(row), b].astype(F32)

    @pl.loop(0, ROWS)
    def _(row):
        weights = [weight_of(row, b) for b in range(BLOCKS)]
        for b in range(BLOCKS):
            lead, lag = weights[b] * lead_in, weights[b] * lag_in
            if b > 0:
                lead = lead + weights[b - 1] * lead_out
            if b < BLOCKS - 1:
                lag = lag + weights[b + 1] * lag_out
            inverse[0, b, row] = 1.0 / jnp.maximum(lead, 1.0)
            inverse[1, b, row] = 1.0 / jnp.maximum(lag, 1.0)

    for edge in (0, BLOCKS + 1):
        weighted[edge] = jnp.zeros((ROWS, BINS, LANES), BF16)

    def integrate(rows, put, first, end):
        held_rows = [rows(first + e) for e in range(4)]
        for t in range(first, end):
            held_rows.append(rows(t + 4))
            total = beams[0] * held_rows[0]
            for j in range(1, 5):
                total = total + beams[j] * held_rows[j]
            put(t, jnp.log(total + 0.05))
            held_rows.pop(0)

    def logs_of(half, place, firsts, ends):
        b, q = block_at(half, place), half * OWN + place

        def rows(e):
            if e < HALO:
                return off[q, HALO - 1 - e].astype(F32)
            if e < HALO + ROWS:
                return power[0, q, e - HALO].astype(F32)
            return on[q, 2 * HALO + ROWS - 1 - e].astype(F32)

        def put(t, value):
            logs[q, t] = value
            row = t - REACH_A
            if 0 <= row < ROWS:
                rounded = value.astype(BF16)
                center[b, row] = rounded
                weighted[b + 1, row] = (
                    rounded.astype(F32) * weight_of(row, b)
                ).astype(BF16)

        integrate(rows, put, firsts[0], ends[0])

        def edge_rows(e):
            if e < 2:
                return off_edge[q, 1 - e].astype(F32)
            if e < 2 + ROWS:
                return power[1, q, e - 2, 0:EDGE].astype(F32)
            return on_edge[q, 1 - (e - 2 - ROWS)].astype(F32)

        waiting = []

        def put_edge(t, value):
            waiting.append(value)
            if t % 2 == 1:
                logs_edge[q, t // 2] = jnp.concatenate(waiting, axis=0).astype(BF16)
                waiting.clear()

        integrate(edge_rows, put_edge, firsts[1], ends[1])

    def level_block(half, place):
        b, q = block_at(half, place), half * OWN + place

        means = []
        for group in range(ROWS // GROUP):
            stacked = jnp.concatenate(
                [
                    center[b, group * GROUP : (group + 1) * GROUP].reshape(
                        GROUP * BINS, LANES
                    ),
                    logs_edge[q, group * GROUP // 2 : (group + 1) * GROUP // 2].reshape(
                        GROUP * EDGE, LANES
                    ),
                ],
                axis=0,
            )
            sums = jnp.dot(doppler, stacked, preferred_element_type=F32)
            size = GROUP * BINS
            means.append(jnp.maximum(sums[:size], sums[size:]))

        far = REACH_A - 2
        lead = logs[q, 0]
        lag = logs[q, REACH_A + 3]
        for d in range(1, far):
            lead = lead + logs[q, d]
            lag = lag + logs[q, REACH_A + 3 + d]
        for row in range(ROWS):
            azimuth = jnp.maximum(
                lead + near_a * logs[q, row + far], lag + near_a * logs[q, row + REACH_A + 2]
            )
            local = row % GROUP
            mean = means[row // GROUP][local * BINS : (local + 1) * BINS]
            level[b, row] = jnp.maximum(azimuth * scale_a, mean * scale_d)
            if row < ROWS - 1:
                lead = lead + (logs[q, row + far] - logs[q, row])
                lag = lag + (logs[q, row + REACH_A + 3 + far] - logs[q, row + REACH_A + 3])

    low = lax.broadcasted_iota(jnp.int32, (8, LANES), 0) < 4

    def finish_block(b):
        cells = pl.ds(pl.multiple_of(b * LANES, LANES), LANES)
        stacked = jnp.concatenate(
            [weighted[b + i].reshape(ROWS * BINS, LANES) for i in range(3)], axis=1
        )
        sums = jnp.dot(stacked, band[...], preferred_element_type=F32)
        for row in range(ROWS):
            here = slice(row * BINS, (row + 1) * BINS)
            lead, lag = inverse[0, b, row], inverse[1, b, row]
            lead = sums[here, :LANES] * jnp.concatenate([lead, lead], axis=0)
            lag = sums[here, LANES:] * jnp.concatenate([lag, lag], axis=0)
            noise = jnp.maximum(jnp.maximum(lead, lag), level[b, row])
            excess = weight_of(row, b) * (center[b, row].astype(F32) - noise)
            first, second = excess[:8], pltpu.roll(excess[8:], 4, 0)
            ordered = jnp.concatenate(
                [jnp.where(low, first, second), jnp.where(low, second, first)], axis=0
            )
            result[physical(row), :, cells] = ordered.astype(BF16)

    def levels(c, half, ends):
        place, size = PIECES[c]

        @pl.loop(0, size)
        def _(index):
            logs_of(half, place + index, (0, 0), ends)
            level_block(half, place + index)

    def finishes(c, half):
        place, size = PIECES[c]
        last = place + size - (c < len(PIECES) - 1)
        for each in range(max(place - 1, 0), last):
            finish_block(block_at(half, each))

    def relay(c):
        if c < len(PIECES):
            receive(c, 0, 1, 2)
            send(c, 9, 10)
        if c + AHEAD < len(PIECES):

            @pl.when(jnp.logical_not(urgent))
            def _():
                send(c + AHEAD, 5, 6)

    for c in range(AHEAD):
        relay(c)

    @pl.when(urgent)
    def _():
        for c in range(AHEAD, len(PIECES)):
            relay(c)

    for c in range(len(PIECES)):
        receive(c, 7, 8)

    @pl.loop(0, OWN)
    def _(place):
        logs_of(rd, place, (HALO, 2), (SPAN, ROWS))

    for c in range(len(PIECES)):
        receive(c, 3, 4)
        send(c, 11, 12)
        receive(c, 9, 10)
        levels(c, rd, (HALO, 2))
        if c > 0:
            finishes(c, rd)

        @pl.when(jnp.logical_not(urgent))
        def _():
            relay(c + AHEAD)

        receive(c, 11, 12, 5, 6)
        levels(c, 1 - rd, (SPAN, ROWS))
        if c == 0:
            finishes(c, rd)
        finishes(c, 1 - rd)

    for c in range(len(PIECES)):
        for kind in range(KINDS):
            transfer(c, kind, rd if kind < PAIR_KINDS + 4 else 1 - rd).wait_send()


def local(echoes, pulse_taper, beam_weights, blanking, cfar_sizes):
    far, near = doppler_bands(GROUP)
    hbm = pl.BlockSpec(memory_space=pltpu.HBM)
    return pl.pallas_call(
        kernel,
        out_shape=jax.ShapeDtypeStruct((ROWS, BINS, BLOCKS * LANES), BF16),
        in_specs=[hbm] * 9,
        out_specs=pl.BlockSpec(memory_space=pltpu.VMEM),
        scratch_shapes=[
            pltpu.VMEM((1, PULSES), F32),
            pltpu.VMEM((2 * PULSES, 2 * PULSES), F32),
            pltpu.VMEM((3 * LANES, 2 * LANES), BF16),
            pltpu.VMEM((2 * GROUP * BINS, GROUP * (BINS + EDGE)), BF16),
            pltpu.VMEM((2 * GROUP * BINS, GROUP * (BINS + EDGE)), BF16),
            pltpu.SMEM((5,), F32),
            pltpu.SMEM((ROWS, BLOCKS), jnp.int32),
            pltpu.SMEM((6,), jnp.int32),
            pltpu.SemaphoreType.DMA((8,)),
            pltpu.VMEM((CHUNKS, 2, ROWS, PULSES, WIDE), BF16),
            pltpu.VMEM((2, BLOCKS, ROWS, BINS, LANES), BF16),
            pltpu.VMEM((BLOCKS, HALO, BINS, LANES), BF16),
            pltpu.VMEM((BLOCKS, 2, EDGE, LANES), BF16),
            pltpu.VMEM((BLOCKS, HALO, BINS, LANES), BF16),
            pltpu.VMEM((BLOCKS, 2, EDGE, LANES), BF16),
            pltpu.VMEM((BLOCKS, SPAN, BINS, LANES), F32),
            pltpu.VMEM((BLOCKS, ROWS // 2, BINS, LANES), BF16),
            pltpu.VMEM((BLOCKS, ROWS, BINS, LANES), BF16),
            pltpu.VMEM((BLOCKS + 2, ROWS, BINS, LANES), BF16),
            pltpu.VMEM((BLOCKS, ROWS, BINS, LANES), F32),
            pltpu.VMEM((2, BLOCKS, ROWS, 8, LANES), F32),
            pltpu.SemaphoreType.DMA((CHUNKS,)),
            pltpu.SemaphoreType.DMA((len(PIECES), KINDS)),
            pltpu.SemaphoreType.DMA((len(PIECES), KINDS)),
        ],
        compiler_params=pltpu.CompilerParams(
            collective_id=0, has_side_effects=True, vmem_limit_bytes=48<<20
        ),
    )(
        *(pltpu.with_memory_space_constraint(x, pltpu.HBM) for x in (
        echoes,
        pulse_taper.reshape(1, PULSES),
        jnp.asarray(trig_table()),
        jnp.asarray(range_band(), BF16),
        jnp.asarray(far, BF16),
        jnp.asarray(near, BF16),
        beam_weights,
        blanking,
        cfar_sizes,
        ))
    )


def solution(mesh):
    in_specs = (P(None, "az", None, "rd"), P(), P(), P("az", None), P())
    out_specs = P("az", "rd", None)
    return jax.shard_map(local, mesh=mesh, in_specs=in_specs, out_specs=out_specs, check_vma=False)
```
